512 devices in a mesh: rep: 16 (over z, x_hi), exp: 32 (over y, x_lo, core).
Axes of the slice: x: 4 (x_hi: 2, x_lo: 2; x = x_hi * 2 + x_lo), y: 8, z: 8, core: 2. Of those that a mesh axis runs over, the one named last changes fastest.
Arguments:
- activations: bfloat16 [65536, 4096], P(('rep', 'exp')), may hold values from -6 to 6
- grad_hidden: bfloat16 [65536, 1024], P(('rep', 'exp')), may hold values from -6 to 6
- pre_gate: bfloat16 [65536, 1024], P(('rep', 'exp')), may hold values from -12 to 12
- pre_up: bfloat16 [65536, 1024], P(('rep', 'exp')), may hold values from -6 to 6
- modality: int32 [65536], P(('rep', 'exp')), may hold values from 0 to 1, as said below
- expert_index: int32 [65536], P(('rep', 'exp')), may hold values from 0 to 1
- master: float32 [16384, 2048], P(('exp', 'rep')), may hold values from -0.09375 to 0.09375
- first_moment: float32 [16384, 2048], P(('exp', 'rep')), may hold values from -18 to 18
- second_moment: float32 [16384, 2048], P(('exp', 'rep')), may hold values from 200 to 2000
Outputs:
- input_grad: bfloat16 [65536, 4096], P(('rep', 'exp'))
- new_master: float32 [16384, 2048], P(('exp', 'rep'))
- new_first: float32 [16384, 2048], P(('exp', 'rep'))
- new_second: float32 [16384, 2048], P(('exp', 'rep'))
The draws below stay inside these ranges and needn't reach their ends.
Inputs may be any that keep to these rules, and one draw needn't show every extreme that they name: Among the 128 tokens of one device no expert 2 * modality + expert_index is named more than 48 times; in every replica group of 4096 tokens one expert is named exactly 48 times on every device.
All inputs are finite; a program needn't handle non-finite values.
Results may differ from the reference program's by a relative error of at most 0.019.
Values may be sent and summed in bfloat16 or wider, within the bound.
No kernel may reach another device: no remote copies, remote signals or barrier semaphores. Data moves between devices by JAX's collectives and lax.ppermute only.
A program may use at most 128 MiB of HBM per device.

```python
import math
import jax
import jax.numpy as jnp

D = 4096
H = 1024
EXPERTS = 4
TOK_DEV = 128
CAP = 48
GROUP_ROWS = 4096
TOKENS = 65536


def route_table(key):
    key = jax.random.fold_in(key, 11)
    blocks = TOKENS // TOK_DEV
    per_group = GROUP_ROWS // TOK_DEV
    key_heavy, key_blocks = jax.random.split(key, 2)
    heavy = jax.random.randint(key_heavy, (TOKENS // GROUP_ROWS,), 0, EXPERTS).astype(jnp.int32)
    heavy_block = jnp.repeat(heavy, per_group, total_repeat_length=blocks)

    def one_block(block_key, top):
        key_pool, key_order = jax.random.split(block_key, 2)
        pool = (jax.random.permutation(key_pool, (EXPERTS - 1) * CAP)[:TOK_DEV - CAP] // CAP).astype(jnp.int32)
        others = pool + (pool >= top).astype(jnp.int32)
        filled = jnp.concatenate([jnp.full((CAP,), top, jnp.int32), others])
        return filled[jax.random.permutation(key_order, TOK_DEV)]
    table = jax.vmap(one_block)(jax.random.split(key_blocks, blocks), heavy_block)
    return table.reshape(TOKENS).astype(jnp.int32)


def draw_modality(key, part):
    return (route_table(key) // (EXPERTS // 2)).astype(jnp.int32)


def draw_expert_index(key, part):
    return (route_table(key) % (EXPERTS // 2)).astype(jnp.int32)


def shard_levels(key, shape, cuts, least, largest):
    def one(axis_at, blocks):
        steps = jax.random.uniform(jax.random.fold_in(jax.random.fold_in(key, 6), axis_at), (blocks,), jnp.float32, least / len(cuts), largest / len(cuts))
        return jnp.repeat(jnp.exp(steps), shape[axis_at] // blocks).reshape((-1,) + (1,) * (len(shape) - axis_at - 1))

    gain = one(*cuts[0])
    for cut in cuts[1:]:
        gain = gain * one(*cut)
    return gain


def gaussian(key, extent, width, bound, shards=(), dtype=jnp.bfloat16):
    loudness = shard_levels(key, extent, shards, -0.22, 0.18) if shards else 1.0
    entries = jax.random.normal(key, extent, jnp.float32) * width * loudness
    return jnp.minimum(jnp.maximum(entries, -bound), bound).astype(dtype)


def setup_inputs(seed: int = 0) -> dict:
    streams_of = jax.random.split(jax.random.key(seed), 10)
    activations = gaussian(streams_of[0], (TOKENS, D), 1.0, 6.0, ((0, 512),))
    grad_hidden = gaussian(streams_of[1], (TOKENS, H), 1.0, 6.0, ((0, 512),))
    pre_gate = gaussian(streams_of[2], (TOKENS, H), 2.0, 12.0, ((0, 512),))
    pre_up = gaussian(streams_of[3], (TOKENS, H), 1.0, 6.0, ((0, 512),))
    modality = draw_modality(jax.random.fold_in(streams_of[9], 71), 0)
    expert_index = draw_expert_index(jax.random.fold_in(streams_of[9], 71), 0)
    master = gaussian(streams_of[6], (EXPERTS * D, 2 * H), D ** -0.5, 0.09375, ((0, 512),), jnp.float32)
    first_moment = gaussian(streams_of[7], (EXPERTS * D, 2 * H), 3.0, 18.0, ((0, 512),), jnp.float32)
    second_moment = jnp.clip(jnp.exp(math.log(2000.0) - 2.3025851 * jax.random.uniform(streams_of[8], (EXPERTS * D, 2 * H), jnp.float32) ** shard_levels(streams_of[8], (EXPERTS * D, 2 * H), ((0, 512),), -0.2, 0.2)), 200.0, 2000.0)
    return {"activations": activations, "grad_hidden": grad_hidden, "pre_gate": pre_gate, "pre_up": pre_up, "modality": modality, "expert_index": expert_index, "master": master, "first_moment": first_moment, "second_moment": second_moment}


beta_one = 0.9
beta_two = 0.999
learn_rate = 0.02
adam_eps = 1e-08
adam_count = 1000

def reference(activations, grad_hidden, pre_gate, pre_up, modality, expert_index, master, first_moment, second_moment):
    expert = (2 * modality + expert_index).astype(jnp.int32)
    gate_val = pre_gate.astype(jnp.float32)
    up_val = pre_up.astype(jnp.float32)
    grad_val = grad_hidden.astype(jnp.float32)
    sig = 1.0 / (1.0 + jnp.exp(-gate_val))
    grad_gate = (grad_val * up_val * sig * (1.0 + gate_val * (1.0 - sig))).astype(jnp.bfloat16)
    grad_up = (grad_val * gate_val * sig).astype(jnp.bfloat16)
    both_grads = jnp.concatenate([grad_gate, grad_up], axis=1)
    weights = master.astype(jnp.bfloat16).reshape(EXPERTS, D, 2 * H)
    input_acc = jnp.zeros((activations.shape[0], D), jnp.float32)
    grad_list = []
    for which in range(EXPERTS):
        chosen = (expert == which)[:, None]
        masked = jnp.where(chosen, both_grads, jnp.zeros_like(both_grads))
        input_acc = input_acc + jnp.dot(masked, weights[which].T, preferred_element_type=jnp.float32)
        grad_list.append(jnp.dot(activations.T, masked, preferred_element_type=jnp.float32))
    input_grad = input_acc.astype(jnp.bfloat16)
    weight_grad = jnp.stack(grad_list, axis=0).reshape(EXPERTS * D, 2 * H)
    new_first = beta_one * first_moment + (1.0 - beta_one) * weight_grad
    new_second = beta_two * second_moment + (1.0 - beta_two) * weight_grad * weight_grad
    corr_one = 1.0 - beta_one ** adam_count
    corr_two = 1.0 - beta_two ** adam_count
    update = new_first / corr_one / (jnp.sqrt(new_second / corr_two) + adam_eps)
    new_master = master - learn_rate * update
    return (input_grad, new_master, new_first, new_second)
```

```python
import jax
import jax.numpy as jnp
from jax import lax
from jax.experimental import pallas as pl
from jax.experimental.pallas import tpu as pltpu
from jax.sharding import Mesh, PartitionSpec as P

EXPERTS = 4
CAP = 48
GROUP = 8

beta_one = 0.9
beta_two = 0.999
learn_rate = 0.02
adam_eps = 1e-08
adam_count = 1000

REP = ("z", "xh")
EXP = ("y", "xl", "core")
ALL = REP + EXP
VMEM = pl.BlockSpec(memory_space=pltpu.VMEM)
BIG = 56 * 1024 * 1024


def params():
    return pltpu.CompilerParams(vmem_limit_bytes=BIG)


def routing_rows(mod_ref, idx_ref):
    expert = 2 * mod_ref[...] + idx_ref[...]
    count = expert.shape[1]
    onehot = (
        lax.broadcasted_iota(jnp.int32, (8, count), 0) == jnp.broadcast_to(expert, (8, count))
    ).astype(jnp.float32)
    earlier = (
        lax.broadcasted_iota(jnp.int32, (count, count), 0)
        < lax.broadcasted_iota(jnp.int32, (count, count), 1)
    ).astype(jnp.float32)
    before = jnp.dot(onehot, earlier, preferred_element_type=jnp.float32)
    pos = jnp.sum(before * onehot, axis=0, keepdims=True).astype(jnp.int32)
    slot = lax.broadcasted_iota(jnp.int32, (CAP, count), 0)
    rows = [
        jnp.where((slot == pos) & (expert == e), 1.0, 0.0).astype(jnp.bfloat16)
        for e in range(EXPERTS)
    ]
    return rows


def pack_grads_kernel(mod_ref, idx_ref, grad_ref, gate_ref, up_ref, out_ref):
    rows = routing_rows(mod_ref, idx_ref)
    routing = jnp.concatenate(rows, axis=0)
    hidden = grad_ref.shape[1]
    piece = out_ref.shape[3]
    for start in range(0, hidden, piece):
        cols = pl.ds(start, piece)
        grad_val = grad_ref[:, cols].astype(jnp.float32)
        gate_val = gate_ref[:, cols].astype(jnp.float32)
        up_val = up_ref[:, cols].astype(jnp.float32)
        sig = 1.0 / (1.0 + jnp.exp(-gate_val))
        grad_gate = (grad_val * up_val * sig * (1.0 + gate_val * (1.0 - sig))).astype(jnp.bfloat16)
        grad_up = (grad_val * gate_val * sig).astype(jnp.bfloat16)
        g = start // piece
        for at, block in ((g, grad_gate), (g + GROUP // 2, grad_up)):
            packed = jnp.dot(routing, block, preferred_element_type=jnp.float32)
            packed = packed.astype(jnp.bfloat16)
            for e in range(EXPERTS):
                out_ref[e, at] = packed[e * CAP : (e + 1) * CAP]


def pack_rows_kernel(mod_ref, idx_ref, x_ref, out_ref):
    rows = routing_rows(mod_ref, idx_ref)
    routing = jnp.concatenate(rows, axis=0)
    piece = out_ref.shape[3]
    for g in range(GROUP):
        block = x_ref[:, g * piece : (g + 1) * piece]
        packed = jnp.dot(routing, block, preferred_element_type=jnp.float32).astype(jnp.bfloat16)
        for e in range(EXPERTS):
            out_ref[e, g] = packed[e * CAP : (e + 1) * CAP]


def combine_kernel(mod_ref, idx_ref, back_ref, out_ref):
    rows = routing_rows(mod_ref, idx_ref)
    routing = jnp.concatenate(rows, axis=0)
    piece = back_ref.shape[3]
    for g in range(GROUP):
        block = jnp.concatenate([back_ref[e, g] for e in range(EXPERTS)], axis=0)
        total = lax.dot_general(
            routing, block, (((0,), (0,)), ((), ())), preferred_element_type=jnp.float32
        )
        out_ref[:, g * piece : (g + 1) * piece] = total.astype(jnp.bfloat16)


def weight_grad_kernel(x_ref, g_ref, out_ref, xt_ref):
    @pl.when(pl.program_id(0) == 0)
    def _():
        xt_ref[...] = x_ref[...].T

    out_ref[...] = jnp.dot(
        xt_ref[...], g_ref[0], preferred_element_type=jnp.float32
    ).astype(jnp.bfloat16)


def input_grad_kernel(g_ref, w_ref, out_ref):
    piece = g_ref.shape[2]
    total = None
    for g in range(GROUP):
        part = lax.dot_general(
            g_ref[g],
            w_ref[:, g * piece : (g + 1) * piece],
            (((1,), (1,)), ((), ())),
            preferred_element_type=jnp.float32,
        )
        total = part if total is None else total + part
    out_ref[...] = total.astype(jnp.bfloat16)


def swap_pairs(count):
    return [(i, i ^ 1) for i in range(count)]


def body(
    activations,
    grad_hidden,
    pre_gate,
    pre_up,
    modality,
    expert_index,
    master,
    first_moment,
    second_moment,
):
    tok_count, width = activations.shape
    hidden = grad_hidden.shape[1]
    piece = width // GROUP
    gpiece = 2 * hidden // GROUP
    members = EXPERTS * GROUP
    rows_total = members * CAP
    mod = modality.reshape(1, tok_count)
    idx = expert_index.reshape(1, tok_count)
    half = lax.axis_index("xh")

    shard_bf = master.astype(jnp.bfloat16)
    pair_bf = lax.all_gather(shard_bf, "xh", axis=0, tiled=True)

    g_send = pl.pallas_call(
        pack_grads_kernel,
        out_shape=jax.ShapeDtypeStruct((EXPERTS, GROUP, CAP, gpiece), jnp.bfloat16),
        in_specs=[VMEM] * 5,
        out_specs=VMEM,
        compiler_params=params(),
        name="pack_grads",
    )(mod, idx, grad_hidden, pre_gate, pre_up)
    weights = lax.all_gather(pair_bf, "z", axis=0, tiled=True)
    g_recv = lax.all_to_all(
        g_send.reshape(members, CAP, gpiece), EXP, split_axis=0, concat_axis=0, tiled=True
    )
    g_mine = g_recv.reshape(rows_total, gpiece)
    g_all = lax.all_gather(
        g_mine,
        EXP,
        axis=0,
        tiled=False,
        axis_index_groups=[list(range(GROUP * e, GROUP * (e + 1))) for e in range(EXPERTS)],
    )
    x_send = pl.pallas_call(
        pack_rows_kernel,
        out_shape=jax.ShapeDtypeStruct((EXPERTS, GROUP, CAP, piece), jnp.bfloat16),
        in_specs=[VMEM] * 3,
        out_specs=VMEM,
        compiler_params=params(),
        name="pack_rows",
    )(mod, idx, activations)
    x_recv = lax.all_to_all(
        x_send.reshape(members, CAP, piece), EXP, split_axis=0, concat_axis=0, tiled=True
    )
    x_rows = x_recv.reshape(rows_total, piece)
    g_all, weights, x_rows = lax.optimization_barrier((g_all, weights, x_rows))

    grad_part = pl.pallas_call(
        weight_grad_kernel,
        grid=(GROUP,),
        out_shape=jax.ShapeDtypeStruct((piece, 2 * hidden), jnp.bfloat16),
        in_specs=[
            pl.BlockSpec((rows_total, piece), lambda g: (0, 0)),
            pl.BlockSpec((1, rows_total, gpiece), lambda g: (g, 0, 0)),
        ],
        out_specs=pl.BlockSpec((piece, gpiece), lambda g: (0, g)),
        scratch_shapes=[pltpu.VMEM((piece, rows_total), jnp.bfloat16)],
        compiler_params=params(),
        name="weight_grad",
    )(x_rows, g_all)
    grad_z = lax.psum_scatter(grad_part, "z", scatter_dimension=0, tiled=True)

    block = 256
    dx_rows = pl.pallas_call(
        input_grad_kernel,
        grid=(rows_total // block,),
        out_shape=jax.ShapeDtypeStruct((rows_total, piece), jnp.bfloat16),
        in_specs=[
            pl.BlockSpec((GROUP, block, gpiece), lambda t: (0, t, 0)),
            pl.BlockSpec((piece, 2 * hidden), lambda t: (0, 0)),
        ],
        out_specs=pl.BlockSpec((block, piece), lambda t: (t, 0)),
        compiler_params=params(),
        name="input_grad",
    )(g_all, weights)
    back = lax.all_to_all(
        dx_rows.reshape(members, CAP, piece), EXP, split_axis=0, concat_axis=0, tiled=True
    )
    input_grad = pl.pallas_call(
        combine_kernel,
        out_shape=jax.ShapeDtypeStruct((tok_count, width), jnp.bfloat16),
        in_specs=[VMEM] * 3,
        out_specs=VMEM,
        compiler_params=params(),
        name="combine",
    )(mod, idx, back.reshape(EXPERTS, GROUP, CAP, piece))

    keep_rows = master.shape[0]
    halves = grad_z.reshape(2, keep_rows, 2 * hidden)
    own = lax.dynamic_index_in_dim(halves, half, 0, keepdims=False)
    other = lax.dynamic_index_in_dim(halves, 1 - half, 0, keepdims=False)
    came = lax.ppermute(other, "xh", swap_pairs(2))
    weight_grad = own.astype(jnp.float32) + came.astype(jnp.float32)
    new_first = beta_one * first_moment + (1.0 - beta_one) * weight_grad
    new_second = beta_two * second_moment + (1.0 - beta_two) * weight_grad * weight_grad
    corr_one = 1.0 - beta_one**adam_count
    corr_two = 1.0 - beta_two**adam_count
    update = new_first / corr_one / (jnp.sqrt(new_second / corr_two) + adam_eps)
    new_master = master - learn_rate * update
    return (input_grad, new_master, new_first, new_second)


def solution(mesh):
    fine = Mesh(mesh.devices.reshape(8, 2, 8, 2, 2), ALL)
    tok = P(ALL, None)
    par = P(EXP + REP, None)
    in_specs = (tok, tok, tok, tok, P(ALL), P(ALL), par, par, par)
    out_specs = (tok, par, par, par)
    return jax.shard_map(body, mesh=fine, in_specs=in_specs, out_specs=out_specs, check_vma=False)
```

```python
import jax
import jax.numpy as jnp
from jax import lax
from jax.experimental import pallas as pl
from jax.experimental.pallas import tpu as pltpu
from jax.sharding import Mesh, PartitionSpec as P

EXPERTS = 4
CAP = 48
GROUP = 8
PIECES = 4

beta_one = 0.9
beta_two = 0.999
learn_rate = 0.02
adam_eps = 1e-08
adam_count = 1000

REP = ("z", "xh")
EXP = ("y", "xl", "core")
ALL = REP + EXP
VMEM = pl.BlockSpec(memory_space=pltpu.VMEM)
BIG = 56 * 1024 * 1024


def params():
    return pltpu.CompilerParams(vmem_limit_bytes=BIG)


def routing_rows(mod_ref, idx_ref):
    expert = 2 * mod_ref[...] + idx_ref[...]
    count = expert.shape[1]
    onehot = (
        lax.broadcasted_iota(jnp.int32, (8, count), 0) == jnp.broadcast_to(expert, (8, count))
    ).astype(jnp.float32)
    earlier = (
        lax.broadcasted_iota(jnp.int32, (count, count), 0)
        < lax.broadcasted_iota(jnp.int32, (count, count), 1)
    ).astype(jnp.float32)
    before = jnp.dot(onehot, earlier, preferred_element_type=jnp.float32)
    pos = jnp.sum(before * onehot, axis=0, keepdims=True).astype(jnp.int32)
    slot = lax.broadcasted_iota(jnp.int32, (CAP, count), 0)
    rows = [
        jnp.where((slot == pos) & (expert == e), 1.0, 0.0).astype(jnp.bfloat16)
        for e in range(EXPERTS)
    ]
    return rows


def pack_grads_kernel(mod_ref, idx_ref, grad_ref, gate_ref, up_ref, out_ref):
    rows = routing_rows(mod_ref, idx_ref)
    routing = jnp.concatenate(rows, axis=0)
    hidden = grad_ref.shape[1]
    piece = out_ref.shape[4]
    for start in range(0, hidden, piece):
        cols = pl.ds(start, piece)
        grad_val = grad_ref[:, cols].astype(jnp.float32)
        gate_val = gate_ref[:, cols].astype(jnp.float32)
        up_val = up_ref[:, cols].astype(jnp.float32)
        sig = 1.0 / (1.0 + jnp.exp(-gate_val))
        grad_gate = (grad_val * up_val * sig * (1.0 + gate_val * (1.0 - sig))).astype(jnp.bfloat16)
        grad_up = (grad_val * gate_val * sig).astype(jnp.bfloat16)
        q = start // piece
        for at, block in ((q, grad_gate), (q + PIECES // 2, grad_up)):
            packed = jnp.dot(routing, block, preferred_element_type=jnp.float32)
            packed = packed.astype(jnp.bfloat16)
            for e in range(EXPERTS):
                for copy in range(GROUP // PIECES):
                    out_ref[e, copy, at] = packed[e * CAP : (e + 1) * CAP]


def pack_rows_kernel(mod_ref, idx_ref, x_ref, out_ref):
    rows = routing_rows(mod_ref, idx_ref)
    routing = jnp.concatenate(rows, axis=0)
    piece = out_ref.shape[3]
    for g in range(GROUP):
        block = x_ref[:, g * piece : (g + 1) * piece]
        packed = jnp.dot(routing, block, preferred_element_type=jnp.float32).astype(jnp.bfloat16)
        for e in range(EXPERTS):
            out_ref[e, g] = packed[e * CAP : (e + 1) * CAP]


def combine_kernel(mod_ref, idx_ref, back_ref, out_ref):
    rows = routing_rows(mod_ref, idx_ref)
    routing = jnp.concatenate(rows, axis=0)
    piece = back_ref.shape[3]
    for g in range(GROUP):
        block = jnp.concatenate([back_ref[e, g] for e in range(EXPERTS)], axis=0)
        total = lax.dot_general(
            routing, block, (((0,), (0,)), ((), ())), preferred_element_type=jnp.float32
        )
        out_ref[:, g * piece : (g + 1) * piece] = total.astype(jnp.bfloat16)


def weight_grad_kernel(q_ref, x_ref, *rest):
    parts = rest[:PIECES]
    out_ref, x_buf, g_buf, xt_buf, sems = rest[PIECES:]
    x_copy = pltpu.make_async_copy(x_ref, x_buf, sems.at[PIECES])
    copies = [pltpu.make_async_copy(parts[j], g_buf.at[j], sems.at[j]) for j in range(PIECES)]
    x_copy.start()
    for copy in copies:
        copy.start()
    x_copy.wait()
    xt_buf[...] = x_buf[...].T
    piece = g_buf.shape[2]
    for j in range(PIECES):
        copies[j].wait()
        at = pl.multiple_of((q_ref[0] ^ j) * piece, piece)
        out_ref[:, pl.ds(at, piece)] = jnp.dot(
            xt_buf[...], g_buf[j], preferred_element_type=jnp.float32
        ).astype(jnp.bfloat16)


def input_grad_kernel(q_ref, *rest):
    parts = rest[:PIECES]
    w_ref, out_ref = rest[PIECES:]
    piece = parts[0].shape[1]
    total = None
    for j in range(PIECES):
        at = pl.multiple_of((q_ref[0] ^ j) * piece, piece)
        part = lax.dot_general(
            parts[j][...],
            w_ref[:, pl.ds(at, piece)],
            (((1,), (1,)), ((), ())),
            preferred_element_type=jnp.float32,
        )
        total = part if total is None else total + part
    out_ref[...] = total.astype(jnp.bfloat16)


def swap_pairs(count):
    return [(i, i ^ 1) for i in range(count)]


def body(
    activations,
    grad_hidden,
    pre_gate,
    pre_up,
    modality,
    expert_index,
    master,
    first_moment,
    second_moment,
):
    tok_count, width = activations.shape
    hidden = grad_hidden.shape[1]
    piece = width // GROUP
    gpiece = 2 * hidden // PIECES
    members = EXPERTS * GROUP
    rows_total = members * CAP
    mod = modality.reshape(1, tok_count)
    idx = expert_index.reshape(1, tok_count)
    half = lax.axis_index("xh")
    spot = (2 * lax.axis_index("xl") + lax.axis_index("core")).astype(jnp.int32).reshape(1)

    g_send = pl.pallas_call(
        pack_grads_kernel,
        out_shape=jax.ShapeDtypeStruct(
            (EXPERTS, GROUP // PIECES, PIECES, CAP, gpiece), jnp.bfloat16
        ),
        in_specs=[VMEM] * 5,
        out_specs=VMEM,
        compiler_params=params(),
        name="pack_grads",
    )(mod, idx, grad_hidden, pre_gate, pre_up)
    g_send, activations, shard = lax.optimization_barrier((g_send, activations, master))
    g_recv = lax.all_to_all(
        g_send.reshape(members, CAP, gpiece), EXP, split_axis=0, concat_axis=0, tiled=True
    )

    own_bf = shard.astype(jnp.bfloat16)
    came_bf = lax.ppermute(own_bf, "xh", swap_pairs(2))
    pair_bf = jnp.where(
        half == 0,
        jnp.concatenate([own_bf, came_bf], axis=0),
        jnp.concatenate([came_bf, own_bf], axis=0),
    )
    weights = lax.all_gather(pair_bf, "z", axis=0, tiled=True)
    x_send = pl.pallas_call(
        pack_rows_kernel,
        out_shape=jax.ShapeDtypeStruct((EXPERTS, GROUP, CAP, piece), jnp.bfloat16),
        in_specs=[VMEM] * 3,
        out_specs=VMEM,
        compiler_params=params(),
        name="pack_rows",
    )(mod, idx, activations)
    g_recv, x_send = lax.optimization_barrier((g_recv, x_send))

    g_own = g_recv.reshape(rows_total, gpiece)
    g_side = lax.ppermute(g_own, "xl", swap_pairs(2))
    g_core = lax.ppermute(g_own, "core", swap_pairs(2))
    g_both = lax.ppermute(g_side, "core", swap_pairs(2))
    pieces = (g_own, g_core, g_side, g_both)

    x_recv = lax.all_to_all(
        x_send.reshape(members, CAP, piece), EXP, split_axis=0, concat_axis=0, tiled=True
    )
    x_rows = x_recv.reshape(rows_total, piece)

    block = 512
    dx_rows = pl.pallas_call(
        input_grad_kernel,
        grid=(rows_total // block,),
        out_shape=jax.ShapeDtypeStruct((rows_total, piece), jnp.bfloat16),
        in_specs=[pl.BlockSpec(memory_space=pltpu.SMEM)]
        + [pl.BlockSpec((block, gpiece), lambda t: (t, 0))] * PIECES
        + [pl.BlockSpec((piece, 2 * hidden), lambda t: (0, 0))],
        out_specs=pl.BlockSpec((block, piece), lambda t: (t, 0)),
        compiler_params=params(),
        name="input_grad",
    )(spot, *pieces, weights)
    dx_rows, x_rows = lax.optimization_barrier((dx_rows, x_rows))

    grad_part = pl.pallas_call(
        weight_grad_kernel,
        out_shape=jax.ShapeDtypeStruct((piece, 2 * hidden), jnp.bfloat16),
        in_specs=[pl.BlockSpec(memory_space=pltpu.SMEM)]
        + [pl.BlockSpec(memory_space=pl.ANY)] * (PIECES + 1),
        out_specs=VMEM,
        scratch_shapes=[
            pltpu.VMEM((rows_total, piece), jnp.bfloat16),
            pltpu.VMEM((PIECES, rows_total, gpiece), jnp.bfloat16),
            pltpu.VMEM((piece, rows_total), jnp.bfloat16),
            pltpu.SemaphoreType.DMA((PIECES + 1,)),
        ],
        compiler_params=params(),
        name="weight_grad",
    )(spot, x_rows, *pieces)
    grad_z = lax.psum_scatter(grad_part, "z", scatter_dimension=0, tiled=True)
    back = lax.all_to_all(
        dx_rows.reshape(members, CAP, piece), EXP, split_axis=0, concat_axis=0, tiled=True
    )
    input_grad = pl.pallas_call(
        combine_kernel,
        out_shape=jax.ShapeDtypeStruct((tok_count, width), jnp.bfloat16),
        in_specs=[VMEM] * 3,
        out_specs=VMEM,
        compiler_params=params(),
        name="combine",
    )(mod, idx, back.reshape(EXPERTS, GROUP, CAP, piece))

    keep_rows = master.shape[0]
    halves = grad_z.reshape(2, keep_rows, 2 * hidden)
    own = lax.dynamic_index_in_dim(halves, half, 0, keepdims=False)
    other = lax.dynamic_index_in_dim(halves, 1 - half, 0, keepdims=False)
    came = lax.ppermute(other, "xh", swap_pairs(2))
    weight_grad = own.astype(jnp.float32) + came.astype(jnp.float32)
    new_first = beta_one * first_moment + (1.0 - beta_one) * weight_grad
    new_second = beta_two * second_moment + (1.0 - beta_two) * weight_grad * weight_grad
    corr_one = 1.0 - beta_one**adam_count
    corr_two = 1.0 - beta_two**adam_count
    update = new_first / corr_one / (jnp.sqrt(new_second / corr_two) + adam_eps)
    new_master = master - learn_rate * update
    return (input_grad, new_master, new_first, new_second)


def solution(mesh):
    fine = Mesh(mesh.devices.reshape(8, 2, 8, 2, 2), ALL)
    tok = P(ALL, None)
    par = P(EXP + REP, None)
    in_specs = (tok, tok, tok, tok, P(ALL), P(ALL), par, par, par)
    out_specs = (tok, par, par, par)
    return jax.shard_map(body, mesh=fine, in_specs=in_specs, out_specs=out_specs, check_vma=False)
```

```python
import jax
import jax.numpy as jnp
from jax import lax
from jax.experimental import pallas as pl
from jax.experimental.pallas import tpu as pltpu
from jax.sharding import Mesh, PartitionSpec as P

EXPERTS = 4
CAP = 48
GROUP = 8
KEEP = 32

beta_one = 0.9
beta_two = 0.999
learn_rate = 0.02
adam_eps = 1e-08
adam_count = 1000

REP = ("z", "xh")
EXP = ("y", "xl", "core")
ALL = REP + EXP
VMEM = pl.BlockSpec(memory_space=pltpu.VMEM)
BIG = 56 * 1024 * 1024


def params():
    return pltpu.CompilerParams(vmem_limit_bytes=BIG)


def routing_rows(mod_ref, idx_ref):
    expert = 2 * mod_ref[...] + idx_ref[...]
    count = expert.shape[1]
    onehot = (
        lax.broadcasted_iota(jnp.int32, (8, count), 0) == jnp.broadcast_to(expert, (8, count))
    ).astype(jnp.float32)
    earlier = (
        lax.broadcasted_iota(jnp.int32, (count, count), 0)
        < lax.broadcasted_iota(jnp.int32, (count, count), 1)
    ).astype(jnp.float32)
    before = jnp.dot(onehot, earlier, preferred_element_type=jnp.float32)
    pos = jnp.sum(before * onehot, axis=0, keepdims=True).astype(jnp.int32)
    slot = lax.broadcasted_iota(jnp.int32, (CAP, count), 0)
    rows = [
        jnp.where((slot == pos) & (expert == e), 1.0, 0.0).astype(jnp.bfloat16)
        for e in range(EXPERTS)
    ]
    return rows


def pack_grads_kernel(mod_ref, idx_ref, grad_ref, gate_ref, up_ref, out_ref):
    rows = routing_rows(mod_ref, idx_ref)
    routing = jnp.concatenate(rows, axis=0)
    hidden = grad_ref.shape[1]
    piece = out_ref.shape[3]
    for start in range(0, hidden, piece):
        cols = pl.ds(start, piece)
        grad_val = grad_ref[:, cols].astype(jnp.float32)
        gate_val = gate_ref[:, cols].astype(jnp.float32)
        up_val = up_ref[:, cols].astype(jnp.float32)
        sig = 1.0 / (1.0 + jnp.exp(-gate_val))
        grad_gate = (grad_val * up_val * sig * (1.0 + gate_val * (1.0 - sig))).astype(jnp.bfloat16)
        grad_up = (grad_val * gate_val * sig).astype(jnp.bfloat16)
        g = start // piece
        for at, block in ((g, grad_gate), (g + GROUP // 2, grad_up)):
            packed = jnp.dot(routing, block, preferred_element_type=jnp.float32)
            packed = packed.astype(jnp.bfloat16)
            for e in range(EXPERTS):
                out_ref[e, at] = packed[e * CAP : (e + 1) * CAP]


def pack_rows_kernel(mod_ref, idx_ref, x_ref, out_ref):
    rows = routing_rows(mod_ref, idx_ref)
    routing = jnp.concatenate(rows, axis=0)
    piece = out_ref.shape[3]
    for g in range(GROUP):
        block = x_ref[:, g * piece : (g + 1) * piece]
        packed = jnp.dot(routing, block, preferred_element_type=jnp.float32).astype(jnp.bfloat16)
        for e in range(EXPERTS):
            out_ref[e, g] = packed[e * CAP : (e + 1) * CAP]


def combine_kernel(mod_ref, idx_ref, back_ref, out_ref):
    rows = routing_rows(mod_ref, idx_ref)
    routing = jnp.concatenate(rows, axis=0)
    piece = back_ref.shape[3]
    for g in range(GROUP):
        block = jnp.concatenate([back_ref[e, g] for e in range(EXPERTS)], axis=0)
        total = lax.dot_general(
            routing, block, (((0,), (0,)), ((), ())), preferred_element_type=jnp.float32
        )
        out_ref[:, g * piece : (g + 1) * piece] = total.astype(jnp.bfloat16)


def weight_grad_kernel(q_ref, x_ref, *rest):
    parts = rest[:GROUP]
    out_ref, x_buf, g_buf, xt_buf, sems = rest[GROUP:]
    x_copy = pltpu.make_async_copy(x_ref, x_buf, sems.at[GROUP])
    copies = [pltpu.make_async_copy(parts[j], g_buf.at[j], sems.at[j]) for j in range(GROUP)]
    x_copy.start()
    for copy in copies:
        copy.start()
    x_copy.wait()
    xt_buf[...] = x_buf[...].T
    piece = g_buf.shape[2]
    for j in range(GROUP):
        copies[j].wait()
        at = pl.multiple_of((q_ref[0] ^ j) * piece, piece)
        block = jnp.dot(
            xt_buf[...], g_buf[j], preferred_element_type=jnp.float32
        ).astype(jnp.bfloat16)
        for r in range(block.shape[0] // KEEP):
            to = pl.multiple_of((r // 2 * 2 + (r % 2 ^ q_ref[1])) * KEEP, KEEP)
            out_ref[pl.ds(to, KEEP), pl.ds(at, piece)] = block[r * KEEP : (r + 1) * KEEP]


def input_grad_kernel(q_ref, *rest):
    parts = rest[:GROUP]
    w_ref, out_ref = rest[GROUP:]
    piece = parts[0].shape[1]
    total = None
    for j in range(GROUP):
        at = pl.multiple_of((q_ref[0] ^ j) * piece, piece)
        part = lax.dot_general(
            parts[j][...],
            w_ref[:, pl.ds(at, piece)],
            (((1,), (1,)), ((), ())),
            preferred_element_type=jnp.float32,
        )
        total = part if total is None else total + part
    out_ref[...] = total.astype(jnp.bfloat16)


def swap_pairs(count):
    return [(i, i ^ 1) for i in range(count)]


def body(
    activations,
    grad_hidden,
    pre_gate,
    pre_up,
    modality,
    expert_index,
    master,
    first_moment,
    second_moment,
):
    tok_count, width = activations.shape
    hidden = grad_hidden.shape[1]
    piece = width // GROUP
    gpiece = 2 * hidden // GROUP
    members = EXPERTS * GROUP
    rows_total = members * CAP
    mod = modality.reshape(1, tok_count)
    idx = expert_index.reshape(1, tok_count)
    half = lax.axis_index("xh")
    member = lax.axis_index(EXP) % GROUP
    spot = jnp.stack([member, half]).astype(jnp.int32)

    g_send = pl.pallas_call(
        pack_grads_kernel,
        out_shape=jax.ShapeDtypeStruct((EXPERTS, GROUP, CAP, gpiece), jnp.bfloat16),
        in_specs=[VMEM] * 5,
        out_specs=VMEM,
        compiler_params=params(),
        name="pack_grads",
    )(mod, idx, grad_hidden, pre_gate, pre_up)
    g_send, activations, shard = lax.optimization_barrier((g_send, activations, master))
    g_recv = lax.all_to_all(
        g_send.reshape(members, CAP, gpiece), EXP, split_axis=0, concat_axis=0, tiled=True
    )

    own_bf = shard.astype(jnp.bfloat16)
    came_bf = lax.ppermute(own_bf, "xh", swap_pairs(2))
    pair_bf = jnp.where(
        half == 0,
        jnp.concatenate([own_bf, came_bf], axis=0),
        jnp.concatenate([came_bf, own_bf], axis=0),
    )
    weights = lax.all_gather(pair_bf, "z", axis=0, tiled=True)
    x_send = pl.pallas_call(
        pack_rows_kernel,
        out_shape=jax.ShapeDtypeStruct((EXPERTS, GROUP, CAP, piece), jnp.bfloat16),
        in_specs=[VMEM] * 3,
        out_specs=VMEM,
        compiler_params=params(),
        name="pack_rows",
    )(mod, idx, activations)
    g_recv, x_send = lax.optimization_barrier((g_recv, x_send))

    g_own = g_recv.reshape(rows_total, gpiece)
    g_y = lax.ppermute(g_own, "y", swap_pairs(8))
    g_x = lax.ppermute(g_own, "xl", swap_pairs(2))
    g_core = lax.ppermute(g_own, "core", swap_pairs(2))
    g_yx = lax.ppermute(g_y, "xl", swap_pairs(2))
    g_x_core = lax.ppermute(g_x, "core", swap_pairs(2))
    g_y_core = lax.ppermute(g_y, "core", swap_pairs(2))
    g_yx_core = lax.ppermute(g_yx, "core", swap_pairs(2))
    pieces = (g_own, g_core, g_x, g_x_core, g_y, g_y_core, g_yx, g_yx_core)

    x_recv = lax.all_to_all(
        x_send.reshape(members, CAP, piece), EXP, split_axis=0, concat_axis=0, tiled=True
    )
    x_rows = x_recv.reshape(rows_total, piece)

    grad_part = pl.pallas_call(
        weight_grad_kernel,
        out_shape=jax.ShapeDtypeStruct((piece, 2 * hidden), jnp.bfloat16),
        in_specs=[pl.BlockSpec(memory_space=pltpu.SMEM)]
        + [pl.BlockSpec(memory_space=pl.ANY)] * (GROUP + 1),
        out_specs=VMEM,
        scratch_shapes=[
            pltpu.VMEM((rows_total, piece), jnp.bfloat16),
            pltpu.VMEM((GROUP, rows_total, gpiece), jnp.bfloat16),
            pltpu.VMEM((piece, rows_total), jnp.bfloat16),
            pltpu.SemaphoreType.DMA((GROUP + 1,)),
        ],
        compiler_params=params(),
        name="weight_grad",
    )(spot, x_rows, *pieces)
    grad_z = lax.psum_scatter(grad_part, "z", scatter_dimension=0, tiled=True)

    grad_part, *pieces = lax.optimization_barrier((grad_part, *pieces))
    block = 512
    dx_rows = pl.pallas_call(
        input_grad_kernel,
        grid=(rows_total // block,),
        out_shape=jax.ShapeDtypeStruct((rows_total, piece), jnp.bfloat16),
        in_specs=[pl.BlockSpec(memory_space=pltpu.SMEM)]
        + [pl.BlockSpec((block, gpiece), lambda t: (t, 0))] * GROUP
        + [pl.BlockSpec((piece, 2 * hidden), lambda t: (0, 0))],
        out_specs=pl.BlockSpec((block, piece), lambda t: (t, 0)),
        compiler_params=params(),
        name="input_grad",
    )(spot, *pieces, weights)
    back = lax.all_to_all(
        dx_rows.reshape(members, CAP, piece), EXP, split_axis=0, concat_axis=0, tiled=True
    )
    input_grad = pl.pallas_call(
        combine_kernel,
        out_shape=jax.ShapeDtypeStruct((tok_count, width), jnp.bfloat16),
        in_specs=[VMEM] * 3,
        out_specs=VMEM,
        compiler_params=params(),
        name="combine",
    )(mod, idx, back.reshape(EXPERTS, GROUP, CAP, piece))

    keep_rows = master.shape[0]
    own = grad_z[:keep_rows]
    other = grad_z[keep_rows:]
    came = lax.ppermute(other, "xh", swap_pairs(2))
    weight_grad = own.astype(jnp.float32) + came.astype(jnp.float32)
    new_first = beta_one * first_moment + (1.0 - beta_one) * weight_grad
    new_second = beta_two * second_moment + (1.0 - beta_two) * weight_grad * weight_grad
    corr_one = 1.0 - beta_one**adam_count
    corr_two = 1.0 - beta_two**adam_count
    update = new_first / corr_one / (jnp.sqrt(new_second / corr_two) + adam_eps)
    new_master = master - learn_rate * update
    return (input_grad, new_master, new_first, new_second)


def solution(mesh):
    fine = Mesh(mesh.devices.reshape(8, 2, 8, 2, 2), ALL)
    tok = P(ALL, None)
    par = P(EXP + REP, None)
    in_specs = (tok, tok, tok, tok, P(ALL), P(ALL), par, par, par)
    out_specs = (tok, par, par, par)
    return jax.shard_map(body, mesh=fine, in_specs=in_specs, out_specs=out_specs, check_vma=False)
```

```python
import functools

import jax
import jax.numpy as jnp
from jax import lax
from jax.experimental import pallas as pl
from jax.experimental.pallas import tpu as pltpu
from jax.sharding import Mesh, PartitionSpec as P

EXPERTS = 4
CAP = 48
GROUP = 8
PIECES = 4

beta_one = 0.9
beta_two = 0.999
learn_rate = 0.02
adam_eps = 1e-08
adam_count = 1000

REP = ("z", "xh")
EXP = ("y", "xl", "core")
ALL = REP + EXP
VMEM = pl.BlockSpec(memory_space=pltpu.VMEM)
BIG = 56 * 1024 * 1024


def params():
    return pltpu.CompilerParams(vmem_limit_bytes=BIG)


def routing_rows(mod_ref, idx_ref):
    expert = 2 * mod_ref[...] + idx_ref[...]
    count = expert.shape[1]
    onehot = (
        lax.broadcasted_iota(jnp.int32, (8, count), 0) == jnp.broadcast_to(expert, (8, count))
    ).astype(jnp.float32)
    earlier = (
        lax.broadcasted_iota(jnp.int32, (count, count), 0)
        < lax.broadcasted_iota(jnp.int32, (count, count), 1)
    ).astype(jnp.float32)
    before = jnp.dot(onehot, earlier, preferred_element_type=jnp.float32)
    pos = jnp.sum(before * onehot, axis=0, keepdims=True).astype(jnp.int32)
    slot = lax.broadcasted_iota(jnp.int32, (CAP, count), 0)
    rows = [
        jnp.where((slot == pos) & (expert == e), 1.0, 0.0).astype(jnp.bfloat16)
        for e in range(EXPERTS)
    ]
    return rows


def pack_grads_kernel(mod_ref, idx_ref, grad_ref, gate_ref, up_ref, out_ref):
    rows = routing_rows(mod_ref, idx_ref)
    routing = jnp.concatenate(rows, axis=0)
    hidden = grad_ref.shape[1]
    piece = out_ref.shape[4]
    for start in range(0, hidden, piece):
        cols = pl.ds(start, piece)
        grad_val = grad_ref[:, cols].astype(jnp.float32)
        gate_val = gate_ref[:, cols].astype(jnp.float32)
        up_val = up_ref[:, cols].astype(jnp.float32)
        sig = 1.0 / (1.0 + jnp.exp(-gate_val))
        grad_gate = (grad_val * up_val * sig * (1.0 + gate_val * (1.0 - sig))).astype(jnp.bfloat16)
        grad_up = (grad_val * gate_val * sig).astype(jnp.bfloat16)
        q = start // piece
        for at, block in ((q, grad_gate), (q + PIECES // 2, grad_up)):
            packed = jnp.dot(routing, block, preferred_element_type=jnp.float32)
            packed = packed.astype(jnp.bfloat16)
            for e in range(EXPERTS):
                for copy in range(GROUP // PIECES):
                    out_ref[e, copy, at] = packed[e * CAP : (e + 1) * CAP]


def pack_rows_kernel(mod_ref, idx_ref, x_ref, out_ref):
    rows = routing_rows(mod_ref, idx_ref)
    routing = jnp.concatenate(rows, axis=0)
    piece = out_ref.shape[3]
    for g in range(GROUP):
        block = x_ref[:, g * piece : (g + 1) * piece]
        packed = jnp.dot(routing, block, preferred_element_type=jnp.float32).astype(jnp.bfloat16)
        for e in range(EXPERTS):
            out_ref[e, g] = packed[e * CAP : (e + 1) * CAP]


def combine_kernel(mod_ref, idx_ref, back_ref, out_ref):
    rows = routing_rows(mod_ref, idx_ref)
    routing = jnp.concatenate(rows, axis=0)
    piece = back_ref.shape[3]
    for g in range(GROUP):
        block = jnp.concatenate([back_ref[e, g] for e in range(EXPERTS)], axis=0)
        total = lax.dot_general(
            routing, block, (((0,), (0,)), ((), ())), preferred_element_type=jnp.float32
        )
        out_ref[:, g * piece : (g + 1) * piece] = total.astype(jnp.bfloat16)


def weight_grad_kernel(slots, first, q_ref, x_ref, *rest):
    count = len(slots)
    parts, rest = rest[:count], rest[count:]
    if first:
        out_ref, xt_ref, x_buf, g_buf, o_buf, sems = rest
    else:
        _, out_ref, xt_ref, g_buf, o_buf, sems = rest
    x_copy = pltpu.make_async_copy(x_ref, x_buf if first else xt_ref, sems.at[2 * count])
    x_copy.start()
    loads = [pltpu.make_async_copy(parts[i], g_buf.at[i], sems.at[i]) for i in range(count)]
    for load in loads:
        load.start()
    x_copy.wait()
    if first:
        xt_ref[...] = x_buf[...].T
    piece = g_buf.shape[2]
    stores = []
    for i, slot in enumerate(slots):
        loads[i].wait()
        o_buf[i] = jnp.dot(
            xt_ref[...], g_buf[i], preferred_element_type=jnp.float32
        ).astype(jnp.bfloat16)
        at = pl.multiple_of((q_ref[0] ^ slot) * piece, piece)
        store = pltpu.make_async_copy(
            o_buf.at[i], out_ref.at[:, pl.ds(at, piece)], sems.at[count + i]
        )
        store.start()
        stores.append(store)
    for store in stores:
        store.wait()


def weight_grad_call(slots, spot, x, parts, done, width):
    first = done is None
    rows, gpiece = parts[0].shape
    piece = x.shape[1] if first else x.shape[0]
    count = len(slots)
    out = jax.ShapeDtypeStruct((piece, width), jnp.bfloat16)
    xt = jax.ShapeDtypeStruct((piece, rows), jnp.bfloat16)
    anywhere = pl.BlockSpec(memory_space=pl.ANY)
    scratch = [
        pltpu.VMEM((rows, piece) if first else (piece, rows), jnp.bfloat16),
        pltpu.VMEM((count, rows, gpiece), jnp.bfloat16),
        pltpu.VMEM((count, piece, gpiece), jnp.bfloat16),
        pltpu.SemaphoreType.DMA((2 * count + 1,)),
    ]
    operands = (spot, x, *parts) if first else (spot, x, *parts, done)
    return pl.pallas_call(
        functools.partial(weight_grad_kernel, slots, first),
        out_shape=(out, xt) if first else out,
        in_specs=[pl.BlockSpec(memory_space=pltpu.SMEM)] + [anywhere] * (len(operands) - 1),
        out_specs=(anywhere, VMEM) if first else anywhere,
        input_output_aliases={} if first else {len(operands) - 1: 0},
        scratch_shapes=scratch,
        compiler_params=params(),
        name="weight_grad",
    )(*operands)


def input_grad_kernel(slots, q_ref, *rest):
    count = len(slots)
    parts, rest = rest[:count], rest[count:]
    w_ref, out_ref = rest[0], rest[-1]
    piece = parts[0].shape[1]
    total = rest[1][...] if len(rest) == 3 else None
    for part_ref, slot in zip(parts, slots):
        at = pl.multiple_of((q_ref[0] ^ slot) * piece, piece)
        part = lax.dot_general(
            part_ref[...],
            w_ref[:, pl.ds(at, piece)],
            (((1,), (1,)), ((), ())),
            preferred_element_type=jnp.float32,
        )
        total = part if total is None else total + part
    out_ref[...] = total.astype(out_ref.dtype)


def input_grad_call(slots, spot, parts, weights, partial):
    rows, gpiece = parts[0].shape
    piece = weights.shape[0]
    block = 512
    by_rows = pl.BlockSpec((block, piece), lambda t: (t, 0))
    extra = [] if partial is None else [partial]
    return pl.pallas_call(
        functools.partial(input_grad_kernel, slots),
        grid=(rows // block,),
        out_shape=jax.ShapeDtypeStruct(
            (rows, piece), jnp.float32 if partial is None else jnp.bfloat16
        ),
        in_specs=[pl.BlockSpec(memory_space=pltpu.SMEM)]
        + [pl.BlockSpec((block, gpiece), lambda t: (t, 0))] * len(parts)
        + [pl.BlockSpec(weights.shape, lambda t: (0, 0))]
        + [by_rows] * len(extra),
        out_specs=by_rows,
        compiler_params=params(),
        name="input_grad",
    )(spot, *parts, weights, *extra)


def swap_pairs(count):
    return [(i, i ^ 1) for i in range(count)]


def body(
    activations,
    grad_hidden,
    pre_gate,
    pre_up,
    modality,
    expert_index,
    master,
    first_moment,
    second_moment,
):
    tok_count, width = activations.shape
    hidden = grad_hidden.shape[1]
    piece = width // GROUP
    gpiece = 2 * hidden // PIECES
    members = EXPERTS * GROUP
    rows_total = members * CAP
    mod = modality.reshape(1, tok_count)
    idx = expert_index.reshape(1, tok_count)
    half = lax.axis_index("xh")
    spot = (2 * lax.axis_index("xl") + lax.axis_index("core")).astype(jnp.int32).reshape(1)

    g_send = pl.pallas_call(
        pack_grads_kernel,
        out_shape=jax.ShapeDtypeStruct(
            (EXPERTS, GROUP // PIECES, PIECES, CAP, gpiece), jnp.bfloat16
        ),
        in_specs=[VMEM] * 5,
        out_specs=VMEM,
        compiler_params=params(),
        name="pack_grads",
    )(mod, idx, grad_hidden, pre_gate, pre_up)
    g_send, activations, shard = lax.optimization_barrier((g_send, activations, master))
    g_recv = lax.all_to_all(
        g_send.reshape(members, CAP, gpiece), EXP, split_axis=0, concat_axis=0, tiled=True
    )

    own_bf = shard.astype(jnp.bfloat16)
    came_bf = lax.ppermute(own_bf, "xh", swap_pairs(2))
    pair_bf = jnp.where(
        half == 0,
        jnp.concatenate([own_bf, came_bf], axis=0),
        jnp.concatenate([came_bf, own_bf], axis=0),
    )
    weights = lax.all_gather(pair_bf, "z", axis=0, tiled=True)
    x_send = pl.pallas_call(
        pack_rows_kernel,
        out_shape=jax.ShapeDtypeStruct((EXPERTS, GROUP, CAP, piece), jnp.bfloat16),
        in_specs=[VMEM] * 3,
        out_specs=VMEM,
        compiler_params=params(),
        name="pack_rows",
    )(mod, idx, activations)
    g_recv, x_send = lax.optimization_barrier((g_recv, x_send))

    g_own = g_recv.reshape(rows_total, gpiece)
    g_side = lax.ppermute(g_own, "xl", swap_pairs(2))
    g_core = lax.ppermute(g_own, "core", swap_pairs(2))

    x_recv = lax.all_to_all(
        x_send.reshape(members, CAP, piece), EXP, split_axis=0, concat_axis=0, tiled=True
    )
    x_rows = x_recv.reshape(rows_total, piece)

    dx_part = input_grad_call((0, 1), spot, (g_own, g_core), weights, None)
    dx_part, g_side = lax.optimization_barrier((dx_part, g_side))
    g_both = lax.ppermute(g_side, "core", swap_pairs(2))
    grad_part, x_turned = weight_grad_call(
        (0, 1), spot, x_rows, (g_own, g_core), None, 2 * hidden
    )
    grad_part = weight_grad_call((2,), spot, x_turned, (g_side,), grad_part, 2 * hidden)
    grad_part = weight_grad_call((3,), spot, x_turned, (g_both,), grad_part, 2 * hidden)
    grad_z = lax.psum_scatter(grad_part, "z", scatter_dimension=0, tiled=True)
    grad_part, dx_part = lax.optimization_barrier((grad_part, dx_part))
    dx_rows = input_grad_call((2, 3), spot, (g_side, g_both), weights, dx_part)
    back = lax.all_to_all(
        dx_rows.reshape(members, CAP, piece), EXP, split_axis=0, concat_axis=0, tiled=True
    )
    input_grad = pl.pallas_call(
        combine_kernel,
        out_shape=jax.ShapeDtypeStruct((tok_count, width), jnp.bfloat16),
        in_specs=[VMEM] * 3,
        out_specs=VMEM,
        compiler_params=params(),
        name="combine",
    )(mod, idx, back.reshape(EXPERTS, GROUP, CAP, piece))

    keep_rows = master.shape[0]
    halves = grad_z.reshape(2, keep_rows, 2 * hidden)
    own = lax.dynamic_index_in_dim(halves, half, 0, keepdims=False)
    other = lax.dynamic_index_in_dim(halves, 1 - half, 0, keepdims=False)
    came = lax.ppermute(other, "xh", swap_pairs(2))
    weight_grad = own.astype(jnp.float32) + came.astype(jnp.float32)
    new_first = beta_one * first_moment + (1.0 - beta_one) * weight_grad
    new_second = beta_two * second_moment + (1.0 - beta_two) * weight_grad * weight_grad
    corr_one = 1.0 - beta_one**adam_count
    corr_two = 1.0 - beta_two**adam_count
    update = new_first / corr_one / (jnp.sqrt(new_second / corr_two) + adam_eps)
    new_master = master - learn_rate * update
    return (input_grad, new_master, new_first, new_second)


def solution(mesh):
    fine = Mesh(mesh.devices.reshape(8, 2, 8, 2, 2), ALL)
    tok = P(ALL, None)
    par = P(EXP + REP, None)
    in_specs = (tok, tok, tok, tok, P(ALL), P(ALL), par, par, par)
    out_specs = (tok, par, par, par)
    return jax.shard_map(body, mesh=fine, in_specs=in_specs, out_specs=out_specs, check_vma=False)
```

```python
import jax
import jax.numpy as jnp
from jax import lax
from jax.experimental import pallas as pl
from jax.experimental.pallas import tpu as pltpu
from jax.sharding import Mesh, PartitionSpec as P

EXPERTS = 4
CAP = 48
GROUP = 8
RING = 8

beta_one = 0.9
beta_two = 0.999
learn_rate = 0.02
adam_eps = 1e-08
adam_count = 1000

REP = ("z", "xh")
EXP = ("y", "xl", "core")
ALL = REP + EXP
VMEM = pl.BlockSpec(memory_space=pltpu.VMEM)
BIG = 56 * 1024 * 1024


def params():
    return pltpu.CompilerParams(vmem_limit_bytes=BIG)


def routing_rows(mod_ref, idx_ref):
    expert = 2 * mod_ref[...] + idx_ref[...]
    count = expert.shape[1]
    onehot = (
        lax.broadcasted_iota(jnp.int32, (8, count), 0) == jnp.broadcast_to(expert, (8, count))
    ).astype(jnp.float32)
    earlier = (
        lax.broadcasted_iota(jnp.int32, (count, count), 0)
        < lax.broadcasted_iota(jnp.int32, (count, count), 1)
    ).astype(jnp.float32)
    before = jnp.dot(onehot, earlier, preferred_element_type=jnp.float32)
    pos = jnp.sum(before * onehot, axis=0, keepdims=True).astype(jnp.int32)
    slot = lax.broadcasted_iota(jnp.int32, (CAP, count), 0)
    rows = [
        jnp.where((slot == pos) & (expert == e), 1.0, 0.0).astype(jnp.bfloat16)
        for e in range(EXPERTS)
    ]
    return rows


def pack_grads_kernel(mod_ref, idx_ref, grad_ref, gate_ref, up_ref, out_ref):
    rows = routing_rows(mod_ref, idx_ref)
    routing = jnp.concatenate(rows, axis=0)
    hidden = grad_ref.shape[1]
    piece = out_ref.shape[3]
    for start in range(0, hidden, piece):
        cols = pl.ds(start, piece)
        grad_val = grad_ref[:, cols].astype(jnp.float32)
        gate_val = gate_ref[:, cols].astype(jnp.float32)
        up_val = up_ref[:, cols].astype(jnp.float32)
        sig = 1.0 / (1.0 + jnp.exp(-gate_val))
        grad_gate = (grad_val * up_val * sig * (1.0 + gate_val * (1.0 - sig))).astype(jnp.bfloat16)
        grad_up = (grad_val * gate_val * sig).astype(jnp.bfloat16)
        g = start // piece
        for at, block in ((g, grad_gate), (g + GROUP // 2, grad_up)):
            packed = jnp.dot(routing, block, preferred_element_type=jnp.float32)
            packed = packed.astype(jnp.bfloat16)
            for e in range(EXPERTS):
                out_ref[e, at] = packed[e * CAP : (e + 1) * CAP]


def pack_rows_kernel(mod_ref, idx_ref, x_ref, out_ref):
    rows = routing_rows(mod_ref, idx_ref)
    routing = jnp.concatenate(rows, axis=0)
    piece = out_ref.shape[3]
    for g in range(GROUP):
        block = x_ref[:, g * piece : (g + 1) * piece]
        packed = jnp.dot(routing, block, preferred_element_type=jnp.float32).astype(jnp.bfloat16)
        for e in range(EXPERTS):
            out_ref[e, g] = packed[e * CAP : (e + 1) * CAP]


def combine_kernel(mod_ref, idx_ref, back_ref, out_ref):
    rows = routing_rows(mod_ref, idx_ref)
    routing = jnp.concatenate(rows, axis=0)
    piece = back_ref.shape[3]
    for g in range(GROUP):
        block = jnp.concatenate([back_ref[e, g] for e in range(EXPERTS)], axis=0)
        total = lax.dot_general(
            routing, block, (((0,), (0,)), ((), ())), preferred_element_type=jnp.float32
        )
        out_ref[:, g * piece : (g + 1) * piece] = total.astype(jnp.bfloat16)


def weight_grad_kernel(x_ref, g_ref, out_ref, x_buf, g_buf, xt_buf, sems):
    pairs = GROUP // 2
    x_copy = pltpu.make_async_copy(x_ref, x_buf, sems.at[pairs])
    copies = [
        pltpu.make_async_copy(g_ref.at[pl.ds(2 * j, 2)], g_buf.at[pl.ds(2 * j, 2)], sems.at[j])
        for j in range(pairs)
    ]
    x_copy.start()
    for copy in copies:
        copy.start()
    x_copy.wait()
    xt_buf[...] = x_buf[...].T
    piece = g_buf.shape[2]
    for j in range(pairs):
        copies[j].wait()
        both = jnp.concatenate([g_buf[2 * j], g_buf[2 * j + 1]], axis=1)
        out_ref[:, 2 * j * piece : (2 * j + 2) * piece] = jnp.dot(
            xt_buf[...], both, preferred_element_type=jnp.float32
        ).astype(jnp.bfloat16)


def input_grad_kernel(z_ref, g_ref, *rest):
    shards, (out_ref, w_buf, sems) = rest[:RING], rest[RING:]
    rows = shards[0].shape[0]

    @pl.when(pl.program_id(0) == 0)
    def _():
        copies = []
        for k in range(RING):
            at = pl.multiple_of(lax.rem(z_ref[0] + RING - k, RING) * rows, rows)
            copies.append(
                pltpu.make_async_copy(shards[k], w_buf.at[pl.ds(at, rows)], sems.at[k])
            )
        for copy in copies:
            copy.start()
        for copy in copies:
            copy.wait()

    grads = jnp.concatenate([g_ref[g] for g in range(GROUP)], axis=1)
    out_ref[...] = lax.dot_general(
        grads, w_buf[...], (((1,), (1,)), ((), ())), preferred_element_type=jnp.float32
    ).astype(jnp.bfloat16)


def swap_pairs(count):
    return [(i, i ^ 1) for i in range(count)]


def body(
    activations,
    grad_hidden,
    pre_gate,
    pre_up,
    modality,
    expert_index,
    master,
    first_moment,
    second_moment,
):
    tok_count, width = activations.shape
    hidden = grad_hidden.shape[1]
    piece = width // GROUP
    gpiece = 2 * hidden // GROUP
    members = EXPERTS * GROUP
    rows_total = members * CAP
    mod = modality.reshape(1, tok_count)
    idx = expert_index.reshape(1, tok_count)
    half = lax.axis_index("xh")
    place = lax.axis_index("z").astype(jnp.int32).reshape(1)

    g_send = pl.pallas_call(
        pack_grads_kernel,
        out_shape=jax.ShapeDtypeStruct((EXPERTS, GROUP, CAP, gpiece), jnp.bfloat16),
        in_specs=[VMEM] * 5,
        out_specs=VMEM,
        compiler_params=params(),
        name="pack_grads",
    )(mod, idx, grad_hidden, pre_gate, pre_up)
    g_send, activations, shard = lax.optimization_barrier((g_send, activations, master))
    g_recv = lax.all_to_all(
        g_send.reshape(members, CAP, gpiece), EXP, split_axis=0, concat_axis=0, tiled=True
    )
    own_bf = shard.astype(jnp.bfloat16)
    came_bf = lax.ppermute(own_bf, "xh", swap_pairs(2))
    pair_bf = jnp.where(
        half == 0,
        jnp.concatenate([own_bf, came_bf], axis=0),
        jnp.concatenate([came_bf, own_bf], axis=0),
    )
    x_send = pl.pallas_call(
        pack_rows_kernel,
        out_shape=jax.ShapeDtypeStruct((EXPERTS, GROUP, CAP, piece), jnp.bfloat16),
        in_specs=[VMEM] * 3,
        out_specs=VMEM,
        compiler_params=params(),
        name="pack_rows",
    )(mod, idx, activations)
    g_recv, x_send, pair_bf = lax.optimization_barrier((g_recv, x_send, pair_bf))
    g_mine = g_recv.reshape(rows_total, gpiece)
    g_all = lax.all_gather(
        g_mine,
        EXP,
        axis=0,
        tiled=False,
        axis_index_groups=[list(range(GROUP * e, GROUP * (e + 1))) for e in range(EXPERTS)],
    )
    x_recv = lax.all_to_all(
        x_send.reshape(members, CAP, piece), EXP, split_axis=0, concat_axis=0, tiled=True
    )
    x_rows = x_recv.reshape(rows_total, piece)
    shards = [pair_bf] + [
        lax.ppermute(pair_bf, "z", [(i, (i + k) % RING) for i in range(RING)])
        for k in range(1, RING)
    ]
    g_all, x_rows, *shards = lax.optimization_barrier((g_all, x_rows, *shards))

    grad_part = pl.pallas_call(
        weight_grad_kernel,
        out_shape=jax.ShapeDtypeStruct((piece, 2 * hidden), jnp.bfloat16),
        in_specs=[pl.BlockSpec(memory_space=pl.ANY)] * 2,
        out_specs=VMEM,
        scratch_shapes=[
            pltpu.VMEM((rows_total, piece), jnp.bfloat16),
            pltpu.VMEM((GROUP, rows_total, gpiece), jnp.bfloat16),
            pltpu.VMEM((piece, rows_total), jnp.bfloat16),
            pltpu.SemaphoreType.DMA((GROUP // 2 + 1,)),
        ],
        compiler_params=params(),
        name="weight_grad",
    )(x_rows, g_all)
    grad_z = lax.psum_scatter(grad_part, "z", scatter_dimension=0, tiled=True)

    grad_part, g_all, *shards = lax.optimization_barrier((grad_part, g_all, *shards))
    block = 512
    dx_rows = pl.pallas_call(
        input_grad_kernel,
        grid=(rows_total // block,),
        out_shape=jax.ShapeDtypeStruct((rows_total, piece), jnp.bfloat16),
        in_specs=[
            pl.BlockSpec(memory_space=pltpu.SMEM),
            pl.BlockSpec((GROUP, block, gpiece), lambda t: (0, t, 0)),
        ]
        + [pl.BlockSpec(memory_space=pl.ANY)] * RING,
        out_specs=pl.BlockSpec((block, piece), lambda t: (t, 0)),
        scratch_shapes=[
            pltpu.VMEM((piece, 2 * hidden), jnp.bfloat16),
            pltpu.SemaphoreType.DMA((RING,)),
        ],
        compiler_params=params(),
        name="input_grad",
    )(place, g_all, *shards)
    back = lax.all_to_all(
        dx_rows.reshape(members, CAP, piece), EXP, split_axis=0, concat_axis=0, tiled=True
    )
    input_grad = pl.pallas_call(
        combine_kernel,
        out_shape=jax.ShapeDtypeStruct((tok_count, width), jnp.bfloat16),
        in_specs=[VMEM] * 3,
        out_specs=VMEM,
        compiler_params=params(),
        name="combine",
    )(mod, idx, back.reshape(EXPERTS, GROUP, CAP, piece))

    keep_rows = master.shape[0]
    halves = grad_z.reshape(2, keep_rows, 2 * hidden)
    own = lax.dynamic_index_in_dim(halves, half, 0, keepdims=False)
    other = lax.dynamic_index_in_dim(halves, 1 - half, 0, keepdims=False)
    came = lax.ppermute(other, "xh", swap_pairs(2))
    weight_grad = own.astype(jnp.float32) + came.astype(jnp.float32)
    new_first = beta_one * first_moment + (1.0 - beta_one) * weight_grad
    new_second = beta_two * second_moment + (1.0 - beta_two) * weight_grad * weight_grad
    corr_one = 1.0 - beta_one**adam_count
    corr_two = 1.0 - beta_two**adam_count
    update = new_first / corr_one / (jnp.sqrt(new_second / corr_two) + adam_eps)
    new_master = master - learn_rate * update
    return (input_grad, new_master, new_first, new_second)


def solution(mesh):
    fine = Mesh(mesh.devices.reshape(8, 2, 8, 2, 2), ALL)
    tok = P(ALL, None)
    par = P(EXP + REP, None)
    in_specs = (tok, tok, tok, tok, P(ALL), P(ALL), par, par, par)
    out_specs = (tok, par, par, par)
    return jax.shard_map(body, mesh=fine, in_specs=in_specs, out_specs=out_specs, check_vma=False)
```

```python
import jax
import jax.numpy as jnp
from jax import lax
from jax.experimental import pallas as pl
from jax.experimental.pallas import tpu as pltpu
from jax.sharding import Mesh, PartitionSpec as P

EXPERTS = 4
CAP = 48
GROUP = 8
RING = 8
DX_BLOCKS = 3
EARLY = (3, 4)

beta_one = 0.9
beta_two = 0.999
learn_rate = 0.02
adam_eps = 1e-08
adam_count = 1000

REP = ("z", "xh")
EXP = ("y", "xl", "core")
ALL = REP + EXP
VMEM = pl.BlockSpec(memory_space=pltpu.VMEM)
BIG = 56 * 1024 * 1024


def params():
    return pltpu.CompilerParams(vmem_limit_bytes=BIG)


def routing_rows(mod_ref, idx_ref):
    expert = 2 * mod_ref[...] + idx_ref[...]
    count = expert.shape[1]
    onehot = (
        lax.broadcasted_iota(jnp.int32, (8, count), 0) == jnp.broadcast_to(expert, (8, count))
    ).astype(jnp.float32)
    earlier = (
        lax.broadcasted_iota(jnp.int32, (count, count), 0)
        < lax.broadcasted_iota(jnp.int32, (count, count), 1)
    ).astype(jnp.float32)
    before = jnp.dot(onehot, earlier, preferred_element_type=jnp.float32)
    pos = jnp.sum(before * onehot, axis=0, keepdims=True).astype(jnp.int32)
    slot = lax.broadcasted_iota(jnp.int32, (CAP, count), 0)
    rows = [
        jnp.where((slot == pos) & (expert == e), 1.0, 0.0).astype(jnp.bfloat16)
        for e in range(EXPERTS)
    ]
    return rows


def pack_grads_kernel(mod_ref, idx_ref, grad_ref, gate_ref, up_ref, out_ref):
    rows = routing_rows(mod_ref, idx_ref)
    routing = jnp.concatenate(rows, axis=0)
    hidden = grad_ref.shape[1]
    piece = out_ref.shape[3]
    for start in range(0, hidden, piece):
        cols = pl.ds(start, piece)
        grad_val = grad_ref[:, cols].astype(jnp.float32)
        gate_val = gate_ref[:, cols].astype(jnp.float32)
        up_val = up_ref[:, cols].astype(jnp.float32)
        sig = 1.0 / (1.0 + jnp.exp(-gate_val))
        grad_gate = (grad_val * up_val * sig * (1.0 + gate_val * (1.0 - sig))).astype(jnp.bfloat16)
        grad_up = (grad_val * gate_val * sig).astype(jnp.bfloat16)
        g = start // piece
        for at, block in ((g, grad_gate), (g + GROUP // 2, grad_up)):
            packed = jnp.dot(routing, block, preferred_element_type=jnp.float32)
            packed = packed.astype(jnp.bfloat16)
            for e in range(EXPERTS):
                out_ref[e, at] = packed[e * CAP : (e + 1) * CAP]


def pack_rows_kernel(mod_ref, idx_ref, x_ref, out_ref):
    rows = routing_rows(mod_ref, idx_ref)
    routing = jnp.concatenate(rows, axis=0)
    piece = out_ref.shape[3]
    for g in range(GROUP):
        block = x_ref[:, g * piece : (g + 1) * piece]
        packed = jnp.dot(routing, block, preferred_element_type=jnp.float32).astype(jnp.bfloat16)
        for e in range(EXPERTS):
            out_ref[e, g] = packed[e * CAP : (e + 1) * CAP]


def combine_kernel(mod_ref, idx_ref, back_ref, out_ref):
    rows = routing_rows(mod_ref, idx_ref)
    routing = jnp.concatenate(rows, axis=0)
    piece = back_ref.shape[3]
    for g in range(GROUP):
        block = jnp.concatenate([back_ref[e, g] for e in range(EXPERTS)], axis=0)
        total = lax.dot_general(
            routing, block, (((0,), (0,)), ((), ())), preferred_element_type=jnp.float32
        )
        out_ref[:, g * piece : (g + 1) * piece] = total.astype(jnp.bfloat16)


def both_grads_kernel(z_ref, x_ref, g_ref, *rest):
    shards, rest = rest[:RING], rest[RING:]
    dw_ref, dx_ref, g_buf, w_buf, xt_buf, dw_buf, dx_buf, g_sems, w_sems, out_sems = rest
    pairs = GROUP // 2
    loads = [
        pltpu.make_async_copy(g_ref.at[pl.ds(2 * j, 2)], g_buf.at[pl.ds(2 * j, 2)], g_sems.at[j])
        for j in range(pairs)
    ]
    rows = shards[0].shape[0]
    w_loads = []
    for k in range(RING):
        at = pl.multiple_of(lax.rem(z_ref[0] + RING - k, RING) * rows, rows)
        w_loads.append(
            pltpu.make_async_copy(shards[k], w_buf.at[pl.ds(at, rows)], w_sems.at[k])
        )
    for load in loads + w_loads:
        load.start()
    xt_buf[...] = x_ref[...].T
    stores = []
    piece = g_buf.shape[2]
    for j in range(pairs):
        loads[j].wait()
        pair = jnp.concatenate([g_buf[2 * j], g_buf[2 * j + 1]], axis=1)
        cols = slice(2 * j * piece, (2 * j + 2) * piece)
        dw_buf[:, cols] = jnp.dot(
            xt_buf[...], pair, preferred_element_type=jnp.float32
        ).astype(jnp.bfloat16)
        stores.append(
            pltpu.make_async_copy(dw_buf.at[:, cols], dw_ref.at[:, cols], out_sems.at[j])
        )
        stores[-1].start()
    for load in w_loads:
        load.wait()
    block = dx_buf.shape[0] // DX_BLOCKS
    for j in range(DX_BLOCKS):
        part = slice(j * block, (j + 1) * block)
        grads = jnp.concatenate([g_buf[g, part] for g in range(GROUP)], axis=1)
        dx_buf[part] = lax.dot_general(
            grads, w_buf[...], (((1,), (1,)), ((), ())), preferred_element_type=jnp.float32
        ).astype(jnp.bfloat16)
        stores.append(
            pltpu.make_async_copy(dx_buf.at[part], dx_ref.at[part], out_sems.at[pairs + j])
        )
        stores[-1].start()
    for store in stores:
        store.wait()


def swap_pairs(count):
    return [(i, i ^ 1) for i in range(count)]


def body(
    activations,
    grad_hidden,
    pre_gate,
    pre_up,
    modality,
    expert_index,
    master,
    first_moment,
    second_moment,
):
    tok_count, width = activations.shape
    hidden = grad_hidden.shape[1]
    piece = width // GROUP
    gpiece = 2 * hidden // GROUP
    members = EXPERTS * GROUP
    rows_total = members * CAP
    mod = modality.reshape(1, tok_count)
    idx = expert_index.reshape(1, tok_count)
    half = lax.axis_index("xh")
    place = lax.axis_index("z").astype(jnp.int32).reshape(1)

    g_send = pl.pallas_call(
        pack_grads_kernel,
        out_shape=jax.ShapeDtypeStruct((EXPERTS, GROUP, CAP, gpiece), jnp.bfloat16),
        in_specs=[VMEM] * 5,
        out_specs=VMEM,
        compiler_params=params(),
        name="pack_grads",
    )(mod, idx, grad_hidden, pre_gate, pre_up)
    g_send, activations, shard = lax.optimization_barrier((g_send, activations, master))
    g_recv = lax.all_to_all(
        g_send.reshape(members, CAP, gpiece), EXP, split_axis=0, concat_axis=0, tiled=True
    )
    own_bf = shard.astype(jnp.bfloat16)
    came_bf = lax.ppermute(own_bf, "xh", swap_pairs(2))
    pair_bf = jnp.where(
        half == 0,
        jnp.concatenate([own_bf, came_bf], axis=0),
        jnp.concatenate([came_bf, own_bf], axis=0),
    )
    x_send = pl.pallas_call(
        pack_rows_kernel,
        out_shape=jax.ShapeDtypeStruct((EXPERTS, GROUP, CAP, piece), jnp.bfloat16),
        in_specs=[VMEM] * 3,
        out_specs=VMEM,
        compiler_params=params(),
        name="pack_rows",
    )(mod, idx, activations)
    g_recv, x_send, pair_late = lax.optimization_barrier((g_recv, x_send, pair_bf))
    g_mine = g_recv.reshape(rows_total, gpiece)
    g_all = lax.all_gather(
        g_mine,
        EXP,
        axis=0,
        tiled=False,
        axis_index_groups=[list(range(GROUP * e, GROUP * (e + 1))) for e in range(EXPERTS)],
    )
    x_recv = lax.all_to_all(
        x_send.reshape(members, CAP, piece), EXP, split_axis=0, concat_axis=0, tiled=True
    )
    x_rows = x_recv.reshape(rows_total, piece)
    shards = [pair_bf]
    for k in range(1, RING):
        moved = pair_bf if k in EARLY else pair_late
        shards.append(lax.ppermute(moved, "z", [(i, (i + k) % RING) for i in range(RING)]))
    g_all, x_rows, *shards = lax.optimization_barrier((g_all, x_rows, *shards))

    anywhere = pl.BlockSpec(memory_space=pl.ANY)
    grad_part, dx_rows = pl.pallas_call(
        both_grads_kernel,
        out_shape=(
            jax.ShapeDtypeStruct((piece, 2 * hidden), jnp.bfloat16),
            jax.ShapeDtypeStruct((rows_total, piece), jnp.bfloat16),
        ),
        in_specs=[pl.BlockSpec(memory_space=pltpu.SMEM), VMEM] + [anywhere] * (RING + 1),
        out_specs=(anywhere, anywhere),
        scratch_shapes=[
            pltpu.VMEM((GROUP, rows_total, gpiece), jnp.bfloat16),
            pltpu.VMEM((piece, 2 * hidden), jnp.bfloat16),
            pltpu.VMEM((piece, rows_total), jnp.bfloat16),
            pltpu.VMEM((piece, 2 * hidden), jnp.bfloat16),
            pltpu.VMEM((rows_total, piece), jnp.bfloat16),
            pltpu.SemaphoreType.DMA((GROUP // 2,)),
            pltpu.SemaphoreType.DMA((RING,)),
            pltpu.SemaphoreType.DMA((GROUP // 2 + DX_BLOCKS,)),
        ],
        compiler_params=params(),
        name="both_grads",
    )(place, pltpu.with_memory_space_constraint(x_rows, pltpu.VMEM), g_all, *shards)
    grad_z = lax.psum_scatter(grad_part, "z", scatter_dimension=0, tiled=True)

    back = lax.all_to_all(
        dx_rows.reshape(members, CAP, piece), EXP, split_axis=0, concat_axis=0, tiled=True
    )
    input_grad = pl.pallas_call(
        combine_kernel,
        out_shape=jax.ShapeDtypeStruct((tok_count, width), jnp.bfloat16),
        in_specs=[VMEM] * 3,
        out_specs=VMEM,
        compiler_params=params(),
        name="combine",
    )(
        mod,
        idx,
        pltpu.with_memory_space_constraint(
            back.reshape(EXPERTS, GROUP, CAP, piece), pltpu.VMEM
        ),
    )

    keep_rows = master.shape[0]
    halves = grad_z.reshape(2, keep_rows, 2 * hidden)
    own = lax.dynamic_index_in_dim(halves, half, 0, keepdims=False)
    other = lax.dynamic_index_in_dim(halves, 1 - half, 0, keepdims=False)
    came = lax.ppermute(other, "xh", swap_pairs(2))
    weight_grad = own.astype(jnp.float32) + came.astype(jnp.float32)
    new_first = beta_one * first_moment + (1.0 - beta_one) * weight_grad
    new_second = beta_two * second_moment + (1.0 - beta_two) * weight_grad * weight_grad
    corr_one = 1.0 - beta_one**adam_count
    corr_two = 1.0 - beta_two**adam_count
    update = new_first / corr_one / (jnp.sqrt(new_second / corr_two) + adam_eps)
    new_master = master - learn_rate * update
    return (input_grad, new_master, new_first, new_second)


def solution(mesh):
    fine = Mesh(mesh.devices.reshape(8, 2, 8, 2, 2), ALL)
    tok = P(ALL, None)
    par = P(EXP + REP, None)
    in_specs = (tok, tok, tok, tok, P(ALL), P(ALL), par, par, par)
    out_specs = (tok, par, par, par)
    return jax.shard_map(body, mesh=fine, in_specs=in_specs, out_specs=out_specs, check_vma=False)
```

```python
import jax
import jax.numpy as jnp
from jax import lax
from jax.experimental import pallas as pl
from jax.experimental.pallas import tpu as pltpu
from jax.sharding import Mesh, PartitionSpec as P

EXPERTS = 4
CAP = 48
GROUP = 8
RING = 8
DX_BLOCKS = 3
EARLY = (3, 4)

beta_one = 0.9
beta_two = 0.999
learn_rate = 0.02
adam_eps = 1e-08
adam_count = 1000

REP = ("z", "xh")
EXP = ("y", "xl", "core")
ALL = REP + EXP
VMEM = pl.BlockSpec(memory_space=pltpu.VMEM)
BIG = 56 * 1024 * 1024


def params():
    return pltpu.CompilerParams(vmem_limit_bytes=BIG)


def routing_rows(mod_ref, idx_ref):
    expert = 2 * mod_ref[...] + idx_ref[...]
    count = expert.shape[1]
    onehot = (
        lax.broadcasted_iota(jnp.int32, (8, count), 0) == jnp.broadcast_to(expert, (8, count))
    ).astype(jnp.float32)
    earlier = (
        lax.broadcasted_iota(jnp.int32, (count, count), 0)
        < lax.broadcasted_iota(jnp.int32, (count, count), 1)
    ).astype(jnp.float32)
    before = jnp.dot(onehot, earlier, preferred_element_type=jnp.float32)
    pos = jnp.sum(before * onehot, axis=0, keepdims=True).astype(jnp.int32)
    slot = lax.broadcasted_iota(jnp.int32, (CAP, count), 0)
    rows = [
        jnp.where((slot == pos) & (expert == e), 1.0, 0.0).astype(jnp.bfloat16)
        for e in range(EXPERTS)
    ]
    return rows


def pack_grads_kernel(mod_ref, idx_ref, grad_ref, gate_ref, up_ref, out_ref):
    rows = routing_rows(mod_ref, idx_ref)
    routing = jnp.concatenate(rows, axis=0)
    hidden = grad_ref.shape[1]
    piece = out_ref.shape[3]
    for start in range(0, hidden, piece):
        cols = pl.ds(start, piece)
        grad_val = grad_ref[:, cols].astype(jnp.float32)
        gate_val = gate_ref[:, cols].astype(jnp.float32)
        up_val = up_ref[:, cols].astype(jnp.float32)
        sig = 1.0 / (1.0 + jnp.exp(-gate_val))
        grad_gate = (grad_val * up_val * sig * (1.0 + gate_val * (1.0 - sig))).astype(jnp.bfloat16)
        grad_up = (grad_val * gate_val * sig).astype(jnp.bfloat16)
        g = start // piece
        for at, block in ((g, grad_gate), (g + GROUP // 2, grad_up)):
            packed = jnp.dot(routing, block, preferred_element_type=jnp.float32)
            packed = packed.astype(jnp.bfloat16)
            for e in range(EXPERTS):
                out_ref[e, at] = packed[e * CAP : (e + 1) * CAP]


def pack_rows_kernel(mod_ref, idx_ref, x_ref, out_ref):
    rows = routing_rows(mod_ref, idx_ref)
    routing = jnp.concatenate(rows, axis=0)
    piece = out_ref.shape[3]
    for g in range(GROUP):
        block = x_ref[:, g * piece : (g + 1) * piece]
        packed = jnp.dot(routing, block, preferred_element_type=jnp.float32).astype(jnp.bfloat16)
        for e in range(EXPERTS):
            out_ref[e, g] = packed[e * CAP : (e + 1) * CAP]


def combine_kernel(mod_ref, idx_ref, back_ref, out_ref):
    rows = routing_rows(mod_ref, idx_ref)
    routing = jnp.concatenate(rows, axis=0)
    piece = back_ref.shape[3]
    for g in range(GROUP):
        block = jnp.concatenate([back_ref[e, g] for e in range(EXPERTS)], axis=0)
        total = lax.dot_general(
            routing, block, (((0,), (0,)), ((), ())), preferred_element_type=jnp.float32
        )
        out_ref[:, g * piece : (g + 1) * piece] = total.astype(jnp.bfloat16)


def weight_grad_kernel(x_ref, g_ref, dw_ref, g_buf, xt_buf, dw_buf, g_sems, out_sems):
    pairs = GROUP // 2
    loads = [
        pltpu.make_async_copy(g_ref.at[pl.ds(2 * j, 2)], g_buf.at[pl.ds(2 * j, 2)], g_sems.at[j])
        for j in range(pairs)
    ]
    for load in loads:
        load.start()
    xt_buf[...] = x_ref[...].T
    stores = []
    piece = g_buf.shape[2]
    for j in range(pairs):
        loads[j].wait()
        pair = jnp.concatenate([g_buf[2 * j], g_buf[2 * j + 1]], axis=1)
        cols = slice(2 * j * piece, (2 * j + 2) * piece)
        dw_buf[:, cols] = jnp.dot(
            xt_buf[...], pair, preferred_element_type=jnp.float32
        ).astype(jnp.bfloat16)
        stores.append(
            pltpu.make_async_copy(dw_buf.at[:, cols], dw_ref.at[:, cols], out_sems.at[j])
        )
        stores[-1].start()
    for store in stores:
        store.wait()


def input_grad_kernel(z_ref, g_ref, *rest):
    shards, rest = rest[:RING], rest[RING:]
    dx_ref, g_buf, w_buf, dx_buf, g_sems, w_sems, out_sems = rest
    rows = shards[0].shape[0]
    w_loads = []
    for k in range(RING):
        at = pl.multiple_of(lax.rem(z_ref[0] + RING - k, RING) * rows, rows)
        w_loads.append(
            pltpu.make_async_copy(shards[k], w_buf.at[pl.ds(at, rows)], w_sems.at[k])
        )
    block = dx_buf.shape[0] // DX_BLOCKS
    parts = [slice(j * block, (j + 1) * block) for j in range(DX_BLOCKS)]
    loads = [
        pltpu.make_async_copy(g_ref.at[:, part], g_buf.at[:, part], g_sems.at[j])
        for j, part in enumerate(parts)
    ]
    for load in w_loads + loads:
        load.start()
    for load in w_loads:
        load.wait()
    stores = []
    for j, part in enumerate(parts):
        loads[j].wait()
        grads = jnp.concatenate([g_buf[g, part] for g in range(GROUP)], axis=1)
        dx_buf[part] = lax.dot_general(
            grads, w_buf[...], (((1,), (1,)), ((), ())), preferred_element_type=jnp.float32
        ).astype(jnp.bfloat16)
        stores.append(pltpu.make_async_copy(dx_buf.at[part], dx_ref.at[part], out_sems.at[j]))
        stores[-1].start()
    for store in stores:
        store.wait()


def swap_pairs(count):
    return [(i, i ^ 1) for i in range(count)]


def body(
    activations,
    grad_hidden,
    pre_gate,
    pre_up,
    modality,
    expert_index,
    master,
    first_moment,
    second_moment,
):
    tok_count, width = activations.shape
    hidden = grad_hidden.shape[1]
    piece = width // GROUP
    gpiece = 2 * hidden // GROUP
    members = EXPERTS * GROUP
    rows_total = members * CAP
    mod = modality.reshape(1, tok_count)
    idx = expert_index.reshape(1, tok_count)
    half = lax.axis_index("xh")
    place = lax.axis_index("z").astype(jnp.int32).reshape(1)

    g_send = pl.pallas_call(
        pack_grads_kernel,
        out_shape=jax.ShapeDtypeStruct((EXPERTS, GROUP, CAP, gpiece), jnp.bfloat16),
        in_specs=[VMEM] * 5,
        out_specs=VMEM,
        compiler_params=params(),
        name="pack_grads",
    )(mod, idx, grad_hidden, pre_gate, pre_up)
    g_send, activations, shard = lax.optimization_barrier((g_send, activations, master))
    g_recv = lax.all_to_all(
        g_send.reshape(members, CAP, gpiece), EXP, split_axis=0, concat_axis=0, tiled=True
    )
    own_bf = shard.astype(jnp.bfloat16)
    came_bf = lax.ppermute(own_bf, "xh", swap_pairs(2))
    pair_bf = jnp.where(
        half == 0,
        jnp.concatenate([own_bf, came_bf], axis=0),
        jnp.concatenate([came_bf, own_bf], axis=0),
    )
    x_send = pl.pallas_call(
        pack_rows_kernel,
        out_shape=jax.ShapeDtypeStruct((EXPERTS, GROUP, CAP, piece), jnp.bfloat16),
        in_specs=[VMEM] * 3,
        out_specs=VMEM,
        compiler_params=params(),
        name="pack_rows",
    )(mod, idx, activations)
    g_recv, x_send, pair_late = lax.optimization_barrier((g_recv, x_send, pair_bf))
    g_mine = g_recv.reshape(rows_total, gpiece)
    g_all = lax.all_gather(
        g_mine,
        EXP,
        axis=0,
        tiled=False,
        axis_index_groups=[list(range(GROUP * e, GROUP * (e + 1))) for e in range(EXPERTS)],
    )
    x_recv = lax.all_to_all(
        x_send.reshape(members, CAP, piece), EXP, split_axis=0, concat_axis=0, tiled=True
    )
    x_rows = x_recv.reshape(rows_total, piece)
    shards = [pair_bf]
    for k in range(1, RING):
        moved = pair_bf if k in EARLY else pair_late
        shards.append(lax.ppermute(moved, "z", [(i, (i + k) % RING) for i in range(RING)]))
    g_all, x_rows, *shards = lax.optimization_barrier((g_all, x_rows, *shards))

    anywhere = pl.BlockSpec(memory_space=pl.ANY)
    grad_part = pl.pallas_call(
        weight_grad_kernel,
        out_shape=jax.ShapeDtypeStruct((piece, 2 * hidden), jnp.bfloat16),
        in_specs=[VMEM, anywhere],
        out_specs=anywhere,
        scratch_shapes=[
            pltpu.VMEM((GROUP, rows_total, gpiece), jnp.bfloat16),
            pltpu.VMEM((piece, rows_total), jnp.bfloat16),
            pltpu.VMEM((piece, 2 * hidden), jnp.bfloat16),
            pltpu.SemaphoreType.DMA((GROUP // 2,)),
            pltpu.SemaphoreType.DMA((GROUP // 2,)),
        ],
        compiler_params=params(),
        name="weight_grad",
    )(pltpu.with_memory_space_constraint(x_rows, pltpu.VMEM), g_all)
    grad_z = lax.psum_scatter(grad_part, "z", scatter_dimension=0, tiled=True)

    grad_part, g_all, *shards = lax.optimization_barrier((grad_part, g_all, *shards))
    dx_rows = pl.pallas_call(
        input_grad_kernel,
        out_shape=jax.ShapeDtypeStruct((rows_total, piece), jnp.bfloat16),
        in_specs=[pl.BlockSpec(memory_space=pltpu.SMEM)] + [anywhere] * (RING + 1),
        out_specs=anywhere,
        scratch_shapes=[
            pltpu.VMEM((GROUP, rows_total, gpiece), jnp.bfloat16),
            pltpu.VMEM((piece, 2 * hidden), jnp.bfloat16),
            pltpu.VMEM((rows_total, piece), jnp.bfloat16),
            pltpu.SemaphoreType.DMA((DX_BLOCKS,)),
            pltpu.SemaphoreType.DMA((RING,)),
            pltpu.SemaphoreType.DMA((DX_BLOCKS,)),
        ],
        compiler_params=params(),
        name="input_grad",
    )(place, g_all, *shards)
    back = lax.all_to_all(
        dx_rows.reshape(members, CAP, piece), EXP, split_axis=0, concat_axis=0, tiled=True
    )
    input_grad = pl.pallas_call(
        combine_kernel,
        out_shape=jax.ShapeDtypeStruct((tok_count, width), jnp.bfloat16),
        in_specs=[VMEM] * 3,
        out_specs=VMEM,
        compiler_params=params(),
        name="combine",
    )(
        mod,
        idx,
        pltpu.with_memory_space_constraint(
            back.reshape(EXPERTS, GROUP, CAP, piece), pltpu.VMEM
        ),
    )

    keep_rows = master.shape[0]
    halves = grad_z.reshape(2, keep_rows, 2 * hidden)
    own = lax.dynamic_index_in_dim(halves, half, 0, keepdims=False)
    other = lax.dynamic_index_in_dim(halves, 1 - half, 0, keepdims=False)
    came = lax.ppermute(other, "xh", swap_pairs(2))
    weight_grad = own.astype(jnp.float32) + came.astype(jnp.float32)
    new_first = beta_one * first_moment + (1.0 - beta_one) * weight_grad
    new_second = beta_two * second_moment + (1.0 - beta_two) * weight_grad * weight_grad
    corr_one = 1.0 - beta_one**adam_count
    corr_two = 1.0 - beta_two**adam_count
    update = new_first / corr_one / (jnp.sqrt(new_second / corr_two) + adam_eps)
    new_master = master - learn_rate * update
    return (input_grad, new_master, new_first, new_second)


def solution(mesh):
    fine = Mesh(mesh.devices.reshape(8, 2, 8, 2, 2), ALL)
    tok = P(ALL, None)
    par = P(EXP + REP, None)
    in_specs = (tok, tok, tok, tok, P(ALL), P(ALL), par, par, par)
    out_specs = (tok, par, par, par)
    return jax.shard_map(body, mesh=fine, in_specs=in_specs, out_specs=out_specs, check_vma=False)
```

```python
import jax
import jax.numpy as jnp
from jax import lax
from jax.experimental import pallas as pl
from jax.experimental.pallas import tpu as pltpu
from jax.sharding import Mesh, PartitionSpec as P

EXPERTS = 4
CAP = 48
GROUP = 8
RING = 8
DX_BLOCKS = 3
EARLY = (3, 4)

beta_one = 0.9
beta_two = 0.999
learn_rate = 0.02
adam_eps = 1e-08
adam_count = 1000

REP = ("z", "xh")
EXP = ("y", "xl", "core")
ALL = REP + EXP
VMEM = pl.BlockSpec(memory_space=pltpu.VMEM)
BIG = 56 * 1024 * 1024
FULL = 63 * 1024 * 1024 + 512 * 1024


def params(limit=BIG):
    return pltpu.CompilerParams(vmem_limit_bytes=limit)


def routing_rows(mod_ref, idx_ref):
    expert = 2 * mod_ref[...] + idx_ref[...]
    count = expert.shape[1]
    onehot = (
        lax.broadcasted_iota(jnp.int32, (8, count), 0) == jnp.broadcast_to(expert, (8, count))
    ).astype(jnp.float32)
    earlier = (
        lax.broadcasted_iota(jnp.int32, (count, count), 0)
        < lax.broadcasted_iota(jnp.int32, (count, count), 1)
    ).astype(jnp.float32)
    before = jnp.dot(onehot, earlier, preferred_element_type=jnp.float32)
    pos = jnp.sum(before * onehot, axis=0, keepdims=True).astype(jnp.int32)
    slot = lax.broadcasted_iota(jnp.int32, (CAP, count), 0)
    rows = [
        jnp.where((slot == pos) & (expert == e), 1.0, 0.0).astype(jnp.bfloat16)
        for e in range(EXPERTS)
    ]
    return rows


def pack_grads_kernel(mod_ref, idx_ref, *rest):
    sources, rest = rest[:3], rest[3:]
    out_ref, in_buf, out_buf, in_sems, out_sems = rest
    hidden = in_buf.shape[2]
    piece = out_buf.shape[3]
    steps = hidden // piece
    loads = []
    for j in range(steps):
        cols = pl.ds(j * piece, piece)
        loads.append(
            [
                pltpu.make_async_copy(
                    sources[i].at[:, cols], in_buf.at[i, :, cols], in_sems.at[3 * j + i]
                )
                for i in range(3)
            ]
        )
    for group in loads:
        for load in group:
            load.start()
    routing = jnp.concatenate(routing_rows(mod_ref, idx_ref), axis=0)
    stores = []
    for j in range(steps):
        for load in loads[j]:
            load.wait()
        cols = pl.ds(j * piece, piece)
        grad_val = in_buf[0, :, cols].astype(jnp.float32)
        gate_val = in_buf[1, :, cols].astype(jnp.float32)
        up_val = in_buf[2, :, cols].astype(jnp.float32)
        sig = 1.0 / (1.0 + jnp.exp(-gate_val))
        grad_gate = (grad_val * up_val * sig * (1.0 + gate_val * (1.0 - sig))).astype(jnp.bfloat16)
        grad_up = (grad_val * gate_val * sig).astype(jnp.bfloat16)
        for at, block in ((j, grad_gate), (j + steps, grad_up)):
            packed = jnp.dot(routing, block, preferred_element_type=jnp.float32)
            packed = packed.astype(jnp.bfloat16)
            for e in range(EXPERTS):
                out_buf[at, e] = packed[e * CAP : (e + 1) * CAP]
            stores.append(
                pltpu.make_async_copy(out_buf.at[at], out_ref.at[:, at], out_sems.at[at])
            )
            stores[-1].start()
    for store in stores:
        store.wait()


def pack_rows_kernel(mod_ref, idx_ref, x_ref, out_ref, routing_ref):
    routing = jnp.concatenate(routing_rows(mod_ref, idx_ref), axis=0)
    routing_ref[...] = routing
    piece = out_ref.shape[3]
    for g in range(GROUP):
        block = x_ref[:, g * piece : (g + 1) * piece]
        packed = jnp.dot(routing, block, preferred_element_type=jnp.float32).astype(jnp.bfloat16)
        for e in range(EXPERTS):
            out_ref[e, g] = packed[e * CAP : (e + 1) * CAP]


def combine_kernel(routing_ref, back_ref, out_ref, out_buf, sems):
    routing = routing_ref[...]
    piece = back_ref.shape[3]
    stores = []
    for g in range(GROUP):
        block = jnp.concatenate([back_ref[e, g] for e in range(EXPERTS)], axis=0)
        total = lax.dot_general(
            routing, block, (((0,), (0,)), ((), ())), preferred_element_type=jnp.float32
        )
        cols = pl.ds(g * piece, piece)
        out_buf[:, cols] = total.astype(jnp.bfloat16)
        stores.append(
            pltpu.make_async_copy(out_buf.at[:, cols], out_ref.at[:, cols], sems.at[g])
        )
        stores[-1].start()
    for store in stores:
        store.wait()


def weight_grad_kernel(x_ref, g_ref, dw_ref, g_buf, xt_buf, dw_buf, g_sems, out_sems):
    pairs = GROUP // 2
    loads = [
        pltpu.make_async_copy(g_ref.at[pl.ds(2 * j, 2)], g_buf.at[pl.ds(2 * j, 2)], g_sems.at[j])
        for j in range(pairs)
    ]
    for load in loads:
        load.start()
    xt_buf[...] = x_ref[...].T
    stores = []
    piece = g_buf.shape[2]
    for j in range(pairs):
        loads[j].wait()
        pair = jnp.concatenate([g_buf[2 * j], g_buf[2 * j + 1]], axis=1)
        cols = slice(2 * j * piece, (2 * j + 2) * piece)
        dw_buf[:, cols] = jnp.dot(
            xt_buf[...], pair, preferred_element_type=jnp.float32
        ).astype(jnp.bfloat16)
        stores.append(
            pltpu.make_async_copy(dw_buf.at[:, cols], dw_ref.at[:, cols], out_sems.at[j])
        )
        stores[-1].start()
    for store in stores:
        store.wait()


def input_grad_kernel(z_ref, g_ref, *rest):
    shards, rest = rest[:RING], rest[RING:]
    dx_ref, g_buf, w_buf, dx_buf, g_sems, w_sems, out_sems = rest
    rows = shards[0].shape[0]
    w_loads = []
    for k in range(RING):
        at = pl.multiple_of(lax.rem(z_ref[0] + RING - k, RING) * rows, rows)
        w_loads.append(
            pltpu.make_async_copy(shards[k], w_buf.at[pl.ds(at, rows)], w_sems.at[k])
        )
    block = dx_buf.shape[0] // DX_BLOCKS
    parts = [slice(j * block, (j + 1) * block) for j in range(DX_BLOCKS)]
    loads = [
        pltpu.make_async_copy(g_ref.at[:, part], g_buf.at[:, part], g_sems.at[j])
        for j, part in enumerate(parts)
    ]
    for load in w_loads + loads:
        load.start()
    for load in w_loads:
        load.wait()
    stores = []
    for j, part in enumerate(parts):
        loads[j].wait()
        grads = jnp.concatenate([g_buf[g, part] for g in range(GROUP)], axis=1)
        dx_buf[part] = lax.dot_general(
            grads, w_buf[...], (((1,), (1,)), ((), ())), preferred_element_type=jnp.float32
        ).astype(jnp.bfloat16)
        stores.append(pltpu.make_async_copy(dx_buf.at[part], dx_ref.at[part], out_sems.at[j]))
        stores[-1].start()
    for store in stores:
        store.wait()


def swap_pairs(count):
    return [(i, i ^ 1) for i in range(count)]


def body(
    activations,
    grad_hidden,
    pre_gate,
    pre_up,
    modality,
    expert_index,
    master,
    first_moment,
    second_moment,
):
    tok_count, width = activations.shape
    hidden = grad_hidden.shape[1]
    piece = width // GROUP
    gpiece = 2 * hidden // GROUP
    members = EXPERTS * GROUP
    rows_total = members * CAP
    mod = modality.reshape(1, tok_count)
    idx = expert_index.reshape(1, tok_count)
    half = lax.axis_index("xh")
    place = lax.axis_index("z").astype(jnp.int32).reshape(1)

    anywhere = pl.BlockSpec(memory_space=pl.ANY)
    g_send = pl.pallas_call(
        pack_grads_kernel,
        out_shape=jax.ShapeDtypeStruct((EXPERTS, GROUP, CAP, gpiece), jnp.bfloat16),
        in_specs=[VMEM] * 2 + [anywhere] * 3,
        out_specs=anywhere,
        scratch_shapes=[
            pltpu.VMEM((3, tok_count, hidden), jnp.bfloat16),
            pltpu.VMEM((GROUP, EXPERTS, CAP, gpiece), jnp.bfloat16),
            pltpu.SemaphoreType.DMA((3 * GROUP // 2,)),
            pltpu.SemaphoreType.DMA((GROUP,)),
        ],
        compiler_params=params(),
        name="pack_grads",
    )(mod, idx, grad_hidden, pre_gate, pre_up)
    g_send, activations, shard = lax.optimization_barrier((g_send, activations, master))
    g_recv = lax.all_to_all(
        g_send.reshape(members, CAP, gpiece), EXP, split_axis=0, concat_axis=0, tiled=True
    )
    own_bf = shard.astype(jnp.bfloat16)
    came_bf = lax.ppermute(own_bf, "xh", swap_pairs(2))
    pair_bf = jnp.where(
        half == 0,
        jnp.concatenate([own_bf, came_bf], axis=0),
        jnp.concatenate([came_bf, own_bf], axis=0),
    )
    x_send, routing = pl.pallas_call(
        pack_rows_kernel,
        out_shape=(
            jax.ShapeDtypeStruct((EXPERTS, GROUP, CAP, piece), jnp.bfloat16),
            jax.ShapeDtypeStruct((EXPERTS * CAP, tok_count), jnp.bfloat16),
        ),
        in_specs=[VMEM] * 3,
        out_specs=(VMEM, VMEM),
        compiler_params=params(FULL),
        name="pack_rows",
    )(mod, idx, activations)
    g_recv, x_send, pair_late = lax.optimization_barrier((g_recv, x_send, pair_bf))
    g_mine = g_recv.reshape(rows_total, gpiece)
    g_all = lax.all_gather(
        g_mine,
        EXP,
        axis=0,
        tiled=False,
        axis_index_groups=[list(range(GROUP * e, GROUP * (e + 1))) for e in range(EXPERTS)],
    )
    x_recv = lax.all_to_all(
        x_send.reshape(members, CAP, piece), EXP, split_axis=0, concat_axis=0, tiled=True
    )
    x_rows = x_recv.reshape(rows_total, piece)
    shards = [pair_bf]
    for k in range(1, RING):
        moved = pair_bf if k in EARLY else pair_late
        shards.append(lax.ppermute(moved, "z", [(i, (i + k) % RING) for i in range(RING)]))
    g_all, x_rows, *shards = lax.optimization_barrier((g_all, x_rows, *shards))

    grad_part = pl.pallas_call(
        weight_grad_kernel,
        out_shape=jax.ShapeDtypeStruct((piece, 2 * hidden), jnp.bfloat16),
        in_specs=[VMEM, anywhere],
        out_specs=anywhere,
        scratch_shapes=[
            pltpu.VMEM((GROUP, rows_total, gpiece), jnp.bfloat16),
            pltpu.VMEM((piece, rows_total), jnp.bfloat16),
            pltpu.VMEM((piece, 2 * hidden), jnp.bfloat16),
            pltpu.SemaphoreType.DMA((GROUP // 2,)),
            pltpu.SemaphoreType.DMA((GROUP // 2,)),
        ],
        compiler_params=params(),
        name="weight_grad",
    )(pltpu.with_memory_space_constraint(x_rows, pltpu.VMEM), g_all)
    grad_z = lax.psum_scatter(grad_part, "z", scatter_dimension=0, tiled=True)

    grad_part, g_all, *shards = lax.optimization_barrier((grad_part, g_all, *shards))
    dx_rows = pl.pallas_call(
        input_grad_kernel,
        out_shape=jax.ShapeDtypeStruct((rows_total, piece), jnp.bfloat16),
        in_specs=[pl.BlockSpec(memory_space=pltpu.SMEM)] + [anywhere] * (RING + 1),
        out_specs=anywhere,
        scratch_shapes=[
            pltpu.VMEM((GROUP, rows_total, gpiece), jnp.bfloat16),
            pltpu.VMEM((piece, 2 * hidden), jnp.bfloat16),
            pltpu.VMEM((rows_total, piece), jnp.bfloat16),
            pltpu.SemaphoreType.DMA((DX_BLOCKS,)),
            pltpu.SemaphoreType.DMA((RING,)),
            pltpu.SemaphoreType.DMA((DX_BLOCKS,)),
        ],
        compiler_params=params(),
        name="input_grad",
    )(place, g_all, *shards)
    back = lax.all_to_all(
        dx_rows.reshape(members, CAP, piece), EXP, split_axis=0, concat_axis=0, tiled=True
    )
    input_grad = pl.pallas_call(
        combine_kernel,
        out_shape=jax.ShapeDtypeStruct((tok_count, width), jnp.bfloat16),
        in_specs=[VMEM] * 2,
        out_specs=anywhere,
        scratch_shapes=[
            pltpu.VMEM((tok_count, width), jnp.bfloat16),
            pltpu.SemaphoreType.DMA((GROUP,)),
        ],
        compiler_params=params(),
        name="combine",
    )(
        routing,
        pltpu.with_memory_space_constraint(
            back.reshape(EXPERTS, GROUP, CAP, piece), pltpu.VMEM
        ),
    )

    keep_rows = master.shape[0]
    halves = grad_z.reshape(2, keep_rows, 2 * hidden)
    own = lax.dynamic_index_in_dim(halves, half, 0, keepdims=False)
    other = lax.dynamic_index_in_dim(halves, 1 - half, 0, keepdims=False)
    came = lax.ppermute(other, "xh", swap_pairs(2))
    weight_grad = own.astype(jnp.float32) + came.astype(jnp.float32)
    new_first = beta_one * first_moment + (1.0 - beta_one) * weight_grad
    new_second = beta_two * second_moment + (1.0 - beta_two) * weight_grad * weight_grad
    corr_one = 1.0 - beta_one**adam_count
    corr_two = 1.0 - beta_two**adam_count
    update = new_first / corr_one / (jnp.sqrt(new_second / corr_two) + adam_eps)
    new_master = master - learn_rate * update
    return (input_grad, new_master, new_first, new_second)


def solution(mesh):
    fine = Mesh(mesh.devices.reshape(8, 2, 8, 2, 2), ALL)
    tok = P(ALL, None)
    par = P(EXP + REP, None)
    in_specs = (tok, tok, tok, tok, P(ALL), P(ALL), par, par, par)
    out_specs = (tok, par, par, par)
    return jax.shard_map(body, mesh=fine, in_specs=in_specs, out_specs=out_specs, check_vma=False)
```

```python
import jax
import jax.numpy as jnp
from jax import lax
from jax.experimental import pallas as pl
from jax.experimental.pallas import tpu as pltpu
from jax.sharding import Mesh, PartitionSpec as P

EXPERTS = 4
CAP = 48
GROUP = 8
RING = 8
DX_BLOCKS = 3
EARLY = (3, 4)

beta_one = 0.9
beta_two = 0.999
learn_rate = 0.02
adam_eps = 1e-08
adam_count = 1000

REP = ("z", "xh")
EXP = ("y", "xl", "core")
ALL = REP + EXP
VMEM = pl.BlockSpec(memory_space=pltpu.VMEM)
BIG = 56 * 1024 * 1024
FULL = 63 * 1024 * 1024 + 512 * 1024


def params(limit=BIG):
    return pltpu.CompilerParams(vmem_limit_bytes=limit)


def routing_rows(mod_ref, idx_ref):
    expert = 2 * mod_ref[...] + idx_ref[...]
    count = expert.shape[1]
    onehot = (
        lax.broadcasted_iota(jnp.int32, (8, count), 0) == jnp.broadcast_to(expert, (8, count))
    ).astype(jnp.float32)
    earlier = (
        lax.broadcasted_iota(jnp.int32, (count, count), 0)
        < lax.broadcasted_iota(jnp.int32, (count, count), 1)
    ).astype(jnp.float32)
    before = jnp.dot(onehot, earlier, preferred_element_type=jnp.float32)
    pos = jnp.sum(before * onehot, axis=0, keepdims=True).astype(jnp.int32)
    slot = lax.broadcasted_iota(jnp.int32, (CAP, count), 0)
    rows = [
        jnp.where((slot == pos) & (expert == e), 1.0, 0.0).astype(jnp.bfloat16)
        for e in range(EXPERTS)
    ]
    return rows


def pack_grads_kernel(mod_ref, idx_ref, grad_ref, gate_ref, up_ref, out_ref):
    rows = routing_rows(mod_ref, idx_ref)
    routing = jnp.concatenate(rows, axis=0)
    hidden = grad_ref.shape[1]
    piece = out_ref.shape[3]
    for start in range(0, hidden, piece):
        cols = pl.ds(start, piece)
        grad_val = grad_ref[:, cols].astype(jnp.float32)
        gate_val = gate_ref[:, cols].astype(jnp.float32)
        up_val = up_ref[:, cols].astype(jnp.float32)
        sig = 1.0 / (1.0 + jnp.exp(-gate_val))
        grad_gate = (grad_val * up_val * sig * (1.0 + gate_val * (1.0 - sig))).astype(jnp.bfloat16)
        grad_up = (grad_val * gate_val * sig).astype(jnp.bfloat16)
        g = start // piece
        for at, block in ((g, grad_gate), (g + GROUP // 2, grad_up)):
            packed = jnp.dot(routing, block, preferred_element_type=jnp.float32)
            packed = packed.astype(jnp.bfloat16)
            for e in range(EXPERTS):
                out_ref[e, at] = packed[e * CAP : (e + 1) * CAP]


def pack_rows_kernel(mod_ref, idx_ref, x_ref, out_ref, routing_ref):
    routing = jnp.concatenate(routing_rows(mod_ref, idx_ref), axis=0)
    routing_ref[...] = routing
    piece = out_ref.shape[3]
    for g in range(GROUP):
        block = x_ref[:, g * piece : (g + 1) * piece]
        packed = jnp.dot(routing, block, preferred_element_type=jnp.float32).astype(jnp.bfloat16)
        for e in range(EXPERTS):
            out_ref[e, g] = packed[e * CAP : (e + 1) * CAP]


def combine_kernel(routing_ref, back_ref, out_ref, out_buf, sems):
    routing = routing_ref[...]
    piece = back_ref.shape[3]
    stores = []
    for g in range(GROUP):
        block = jnp.concatenate([back_ref[e, g] for e in range(EXPERTS)], axis=0)
        total = lax.dot_general(
            routing, block, (((0,), (0,)), ((), ())), preferred_element_type=jnp.float32
        )
        cols = pl.ds(g * piece, piece)
        out_buf[:, cols] = total.astype(jnp.bfloat16)
        stores.append(
            pltpu.make_async_copy(out_buf.at[:, cols], out_ref.at[:, cols], sems.at[g])
        )
        stores[-1].start()
    for store in stores:
        store.wait()


def turn_kernel(x_ref, xt_ref):
    xt_ref[...] = x_ref[...].T


def weight_grad_kernel(xt_ref, g_ref, dw_ref, g_buf, dw_buf, g_sems, out_sems):
    pairs = GROUP // 2
    loads = [
        pltpu.make_async_copy(g_ref.at[pl.ds(2 * j, 2)], g_buf.at[pl.ds(2 * j, 2)], g_sems.at[j])
        for j in range(pairs)
    ]
    for load in loads:
        load.start()
    stores = []
    piece = g_buf.shape[2]
    for j in range(pairs):
        loads[j].wait()
        pair = jnp.concatenate([g_buf[2 * j], g_buf[2 * j + 1]], axis=1)
        cols = slice(2 * j * piece, (2 * j + 2) * piece)
        dw_buf[:, cols] = jnp.dot(
            xt_ref[...], pair, preferred_element_type=jnp.float32
        ).astype(jnp.bfloat16)
        stores.append(
            pltpu.make_async_copy(dw_buf.at[:, cols], dw_ref.at[:, cols], out_sems.at[j])
        )
        stores[-1].start()
    for store in stores:
        store.wait()


def input_grad_kernel(z_ref, g_ref, *rest):
    shards, rest = rest[:RING], rest[RING:]
    dx_ref, g_buf, w_buf, dx_buf, g_sems, w_sems, out_sems = rest
    rows = shards[0].shape[0]
    w_loads = []
    for k in range(RING):
        at = pl.multiple_of(lax.rem(z_ref[0] + RING - k, RING) * rows, rows)
        w_loads.append(
            pltpu.make_async_copy(shards[k], w_buf.at[pl.ds(at, rows)], w_sems.at[k])
        )
    block = dx_buf.shape[0] // DX_BLOCKS
    parts = [slice(j * block, (j + 1) * block) for j in range(DX_BLOCKS)]
    loads = [
        pltpu.make_async_copy(g_ref.at[:, part], g_buf.at[:, part], g_sems.at[j])
        for j, part in enumerate(parts)
    ]
    for load in w_loads + loads:
        load.start()
    for load in w_loads:
        load.wait()
    stores = []
    for j, part in enumerate(parts):
        loads[j].wait()
        grads = jnp.concatenate([g_buf[g, part] for g in range(GROUP)], axis=1)
        dx_buf[part] = lax.dot_general(
            grads, w_buf[...], (((1,), (1,)), ((), ())), preferred_element_type=jnp.float32
        ).astype(jnp.bfloat16)
        stores.append(pltpu.make_async_copy(dx_buf.at[part], dx_ref.at[part], out_sems.at[j]))
        stores[-1].start()
    for store in stores:
        store.wait()


def swap_pairs(count):
    return [(i, i ^ 1) for i in range(count)]


def body(
    activations,
    grad_hidden,
    pre_gate,
    pre_up,
    modality,
    expert_index,
    master,
    first_moment,
    second_moment,
):
    tok_count, width = activations.shape
    hidden = grad_hidden.shape[1]
    piece = width // GROUP
    gpiece = 2 * hidden // GROUP
    members = EXPERTS * GROUP
    rows_total = members * CAP
    mod = modality.reshape(1, tok_count)
    idx = expert_index.reshape(1, tok_count)
    half = lax.axis_index("xh")
    place = lax.axis_index("z").astype(jnp.int32).reshape(1)

    anywhere = pl.BlockSpec(memory_space=pl.ANY)
    anywhere = pl.BlockSpec(memory_space=pl.ANY)
    g_send = pl.pallas_call(
        pack_grads_kernel,
        out_shape=jax.ShapeDtypeStruct((EXPERTS, GROUP, CAP, gpiece), jnp.bfloat16),
        in_specs=[VMEM] * 5,
        out_specs=VMEM,
        compiler_params=params(),
        name="pack_grads",
    )(mod, idx, grad_hidden, pre_gate, pre_up)
    g_send, activations, shard = lax.optimization_barrier((g_send, activations, master))
    g_recv = lax.all_to_all(
        g_send.reshape(members, CAP, gpiece), EXP, split_axis=0, concat_axis=0, tiled=True
    )
    own_bf = shard.astype(jnp.bfloat16)
    came_bf = lax.ppermute(own_bf, "xh", swap_pairs(2))
    pair_bf = jnp.where(
        half == 0,
        jnp.concatenate([own_bf, came_bf], axis=0),
        jnp.concatenate([came_bf, own_bf], axis=0),
    )
    x_send, routing = pl.pallas_call(
        pack_rows_kernel,
        out_shape=(
            jax.ShapeDtypeStruct((EXPERTS, GROUP, CAP, piece), jnp.bfloat16),
            jax.ShapeDtypeStruct((EXPERTS * CAP, tok_count), jnp.bfloat16),
        ),
        in_specs=[VMEM] * 3,
        out_specs=(VMEM, VMEM),
        compiler_params=params(FULL),
        name="pack_rows",
    )(mod, idx, activations)
    g_recv, x_send, pair_late = lax.optimization_barrier((g_recv, x_send, pair_bf))
    g_mine = g_recv.reshape(rows_total, gpiece)
    g_all = lax.all_gather(
        g_mine,
        EXP,
        axis=0,
        tiled=False,
        axis_index_groups=[list(range(GROUP * e, GROUP * (e + 1))) for e in range(EXPERTS)],
    )
    x_recv = lax.all_to_all(
        x_send.reshape(members, CAP, piece), EXP, split_axis=0, concat_axis=0, tiled=True
    )
    x_rows = x_recv.reshape(rows_total, piece)
    shards = [pair_bf]
    for k in range(1, RING):
        moved = pair_bf if k in EARLY else pair_late
        shards.append(lax.ppermute(moved, "z", [(i, (i + k) % RING) for i in range(RING)]))
    x_turned = pl.pallas_call(
        turn_kernel,
        out_shape=pltpu.VMEM((piece, rows_total), jnp.bfloat16),
        in_specs=[VMEM],
        out_specs=VMEM,
        compiler_params=params(),
        name="turn",
    )(pltpu.with_memory_space_constraint(x_rows, pltpu.VMEM))
    g_all, *shards = lax.optimization_barrier((g_all, *shards))

    grad_part = pl.pallas_call(
        weight_grad_kernel,
        out_shape=jax.ShapeDtypeStruct((piece, 2 * hidden), jnp.bfloat16),
        in_specs=[VMEM, anywhere],
        out_specs=anywhere,
        scratch_shapes=[
            pltpu.VMEM((GROUP, rows_total, gpiece), jnp.bfloat16),
            pltpu.VMEM((piece, 2 * hidden), jnp.bfloat16),
            pltpu.SemaphoreType.DMA((GROUP // 2,)),
            pltpu.SemaphoreType.DMA((GROUP // 2,)),
        ],
        compiler_params=params(),
        name="weight_grad",
    )(pltpu.with_memory_space_constraint(x_turned, pltpu.VMEM), g_all)
    grad_z = lax.psum_scatter(grad_part, "z", scatter_dimension=0, tiled=True)

    grad_part, g_all, *shards = lax.optimization_barrier((grad_part, g_all, *shards))
    dx_rows = pl.pallas_call(
        input_grad_kernel,
        out_shape=jax.ShapeDtypeStruct((rows_total, piece), jnp.bfloat16),
        in_specs=[pl.BlockSpec(memory_space=pltpu.SMEM)] + [anywhere] * (RING + 1),
        out_specs=anywhere,
        scratch_shapes=[
            pltpu.VMEM((GROUP, rows_total, gpiece), jnp.bfloat16),
            pltpu.VMEM((piece, 2 * hidden), jnp.bfloat16),
            pltpu.VMEM((rows_total, piece), jnp.bfloat16),
            pltpu.SemaphoreType.DMA((DX_BLOCKS,)),
            pltpu.SemaphoreType.DMA((RING,)),
            pltpu.SemaphoreType.DMA((DX_BLOCKS,)),
        ],
        compiler_params=params(),
        name="input_grad",
    )(place, g_all, *shards)
    back = lax.all_to_all(
        dx_rows.reshape(members, CAP, piece), EXP, split_axis=0, concat_axis=0, tiled=True
    )
    input_grad = pl.pallas_call(
        combine_kernel,
        out_shape=jax.ShapeDtypeStruct((tok_count, width), jnp.bfloat16),
        in_specs=[VMEM] * 2,
        out_specs=anywhere,
        scratch_shapes=[
            pltpu.VMEM((tok_count, width), jnp.bfloat16),
            pltpu.SemaphoreType.DMA((GROUP,)),
        ],
        compiler_params=params(),
        name="combine",
    )(
        routing,
        pltpu.with_memory_space_constraint(
            back.reshape(EXPERTS, GROUP, CAP, piece), pltpu.VMEM
        ),
    )

    keep_rows = master.shape[0]
    halves = grad_z.reshape(2, keep_rows, 2 * hidden)
    own = lax.dynamic_index_in_dim(halves, half, 0, keepdims=False)
    other = lax.dynamic_index_in_dim(halves, 1 - half, 0, keepdims=False)
    came = lax.ppermute(other, "xh", swap_pairs(2))
    weight_grad = own.astype(jnp.float32) + came.astype(jnp.float32)
    new_first = beta_one * first_moment + (1.0 - beta_one) * weight_grad
    new_second = beta_two * second_moment + (1.0 - beta_two) * weight_grad * weight_grad
    corr_one = 1.0 - beta_one**adam_count
    corr_two = 1.0 - beta_two**adam_count
    update = new_first / corr_one / (jnp.sqrt(new_second / corr_two) + adam_eps)
    new_master = master - learn_rate * update
    return (input_grad, new_master, new_first, new_second)


def solution(mesh):
    fine = Mesh(mesh.devices.reshape(8, 2, 8, 2, 2), ALL)
    tok = P(ALL, None)
    par = P(EXP + REP, None)
    in_specs = (tok, tok, tok, tok, P(ALL), P(ALL), par, par, par)
    out_specs = (tok, par, par, par)
    return jax.shard_map(body, mesh=fine, in_specs=in_specs, out_specs=out_specs, check_vma=False)
```

```python
import jax
import jax.numpy as jnp
from jax import lax
from jax.experimental import pallas as pl
from jax.experimental.pallas import tpu as pltpu
from jax.sharding import Mesh, PartitionSpec as P

EXPERTS = 4
CAP = 48
GROUP = 8
RING = 8
DX_BLOCKS = 3
EARLY = (3, 4)

beta_one = 0.9
beta_two = 0.999
learn_rate = 0.02
adam_eps = 1e-08
adam_count = 1000

REP = ("z", "xh")
EXP = ("y", "xl", "core")
ALL = REP + EXP
VMEM = pl.BlockSpec(memory_space=pltpu.VMEM)
BIG = 56 * 1024 * 1024
FULL = 63 * 1024 * 1024 + 512 * 1024


def params(limit=BIG):
    return pltpu.CompilerParams(vmem_limit_bytes=limit)


def routing_rows(mod_ref, idx_ref):
    expert = 2 * mod_ref[...] + idx_ref[...]
    count = expert.shape[1]
    onehot = (
        lax.broadcasted_iota(jnp.int32, (8, count), 0) == jnp.broadcast_to(expert, (8, count))
    ).astype(jnp.bfloat16)
    earlier = (
        lax.broadcasted_iota(jnp.int32, (count, count), 0)
        < lax.broadcasted_iota(jnp.int32, (count, count), 1)
    ).astype(jnp.bfloat16)
    before = jnp.dot(onehot, earlier, preferred_element_type=jnp.float32)
    pos = jnp.sum(before * onehot.astype(jnp.float32), axis=0, keepdims=True).astype(jnp.int32)
    slot = lax.broadcasted_iota(jnp.int32, (CAP, count), 0)
    rows = [
        jnp.where((slot == pos) & (expert == e), 1.0, 0.0).astype(jnp.bfloat16)
        for e in range(EXPERTS)
    ]
    return rows


def pack_grads_kernel(mod_ref, idx_ref, grad_ref, gate_ref, up_ref, out_ref):
    rows = routing_rows(mod_ref, idx_ref)
    routing = jnp.concatenate(rows, axis=0)
    hidden = grad_ref.shape[1]
    piece = out_ref.shape[3]
    for start in range(0, hidden, piece):
        cols = pl.ds(start, piece)
        grad_val = grad_ref[:, cols].astype(jnp.float32)
        gate_val = gate_ref[:, cols].astype(jnp.float32)
        up_val = up_ref[:, cols].astype(jnp.float32)
        sig = 1.0 / (1.0 + jnp.exp(-gate_val))
        grad_gate = (grad_val * up_val * sig * (1.0 + gate_val * (1.0 - sig))).astype(jnp.bfloat16)
        grad_up = (grad_val * gate_val * sig).astype(jnp.bfloat16)
        g = start // piece
        for at, block in ((g, grad_gate), (g + GROUP // 2, grad_up)):
            packed = jnp.dot(routing, block, preferred_element_type=jnp.float32)
            packed = packed.astype(jnp.bfloat16)
            for e in range(EXPERTS):
                out_ref[e, at] = packed[e * CAP : (e + 1) * CAP]


def pack_rows_kernel(mod_ref, idx_ref, x_ref, out_ref, routing_ref):
    routing = jnp.concatenate(routing_rows(mod_ref, idx_ref), axis=0)
    routing_ref[...] = routing
    piece = out_ref.shape[3]
    for g in range(GROUP):
        block = x_ref[:, g * piece : (g + 1) * piece]
        packed = jnp.dot(routing, block, preferred_element_type=jnp.float32).astype(jnp.bfloat16)
        for e in range(EXPERTS):
            out_ref[e, g] = packed[e * CAP : (e + 1) * CAP]


def combine_kernel(routing_ref, back_ref, out_ref, out_buf, sems):
    routing = routing_ref[...]
    piece = back_ref.shape[3]
    stores = []
    for g in range(GROUP):
        block = jnp.concatenate([back_ref[e, g] for e in range(EXPERTS)], axis=0)
        total = lax.dot_general(
            routing, block, (((0,), (0,)), ((), ())), preferred_element_type=jnp.float32
        )
        cols = pl.ds(g * piece, piece)
        out_buf[:, cols] = total.astype(jnp.bfloat16)
        stores.append(
            pltpu.make_async_copy(out_buf.at[:, cols], out_ref.at[:, cols], sems.at[g])
        )
        stores[-1].start()
    for store in stores:
        store.wait()


def turn_kernel(x_ref, xt_ref):
    xt_ref[...] = x_ref[...].T


def weight_grad_kernel(xt_ref, g_ref, dw_ref, g_buf, dw_buf, g_sems, out_sems):
    pairs = GROUP // 2
    loads = [
        pltpu.make_async_copy(g_ref.at[pl.ds(2 * j, 2)], g_buf.at[pl.ds(2 * j, 2)], g_sems.at[j])
        for j in range(pairs)
    ]
    for load in loads[:-1]:
        load.start()
    stores = []
    piece = g_buf.shape[2]
    for j in range(pairs):
        loads[j].wait()
        if j == 0:
            loads[-1].start()
        pair = jnp.concatenate([g_buf[2 * j], g_buf[2 * j + 1]], axis=1)
        cols = slice(2 * j * piece, (2 * j + 2) * piece)
        dw_buf[:, cols] = jnp.dot(
            xt_ref[...], pair, preferred_element_type=jnp.float32
        ).astype(jnp.bfloat16)
        stores.append(
            pltpu.make_async_copy(dw_buf.at[:, cols], dw_ref.at[:, cols], out_sems.at[j])
        )
        stores[-1].start()
    for store in stores:
        store.wait()


def input_grad_kernel(z_ref, g_ref, *rest):
    shards, rest = rest[:RING], rest[RING:]
    dx_ref, g_buf, w_buf, dx_buf, g_sems, w_sems, out_sems = rest
    rows = shards[0].shape[0]
    w_loads = []
    for k in range(RING):
        at = pl.multiple_of(lax.rem(z_ref[0] + RING - k, RING) * rows, rows)
        w_loads.append(
            pltpu.make_async_copy(shards[k], w_buf.at[pl.ds(at, rows)], w_sems.at[k])
        )
    total = dx_buf.shape[0]
    edges = [0, total // 6, total * 7 // 12, total]
    parts = [slice(edges[j], edges[j + 1]) for j in range(DX_BLOCKS)]
    loads = [
        pltpu.make_async_copy(g_ref.at[:, part], g_buf.at[:, part], g_sems.at[j])
        for j, part in enumerate(parts)
    ]
    for load in w_loads + loads[:-1]:
        load.start()
    for load in w_loads:
        load.wait()
    stores = []
    for j, part in enumerate(parts):
        loads[j].wait()
        if j == 0:
            loads[-1].start()
        grads = jnp.concatenate([g_buf[g, part] for g in range(GROUP)], axis=1)
        dx_buf[part] = lax.dot_general(
            grads, w_buf[...], (((1,), (1,)), ((), ())), preferred_element_type=jnp.float32
        ).astype(jnp.bfloat16)
        stores.append(pltpu.make_async_copy(dx_buf.at[part], dx_ref.at[part], out_sems.at[j]))
        stores[-1].start()
    for store in stores:
        store.wait()


def swap_pairs(count):
    return [(i, i ^ 1) for i in range(count)]


def body(
    activations,
    grad_hidden,
    pre_gate,
    pre_up,
    modality,
    expert_index,
    master,
    first_moment,
    second_moment,
):
    tok_count, width = activations.shape
    hidden = grad_hidden.shape[1]
    piece = width // GROUP
    gpiece = 2 * hidden // GROUP
    members = EXPERTS * GROUP
    rows_total = members * CAP
    mod = modality.reshape(1, tok_count)
    idx = expert_index.reshape(1, tok_count)
    half = lax.axis_index("xh")
    place = lax.axis_index("z").astype(jnp.int32).reshape(1)

    anywhere = pl.BlockSpec(memory_space=pl.ANY)
    anywhere = pl.BlockSpec(memory_space=pl.ANY)
    g_send = pl.pallas_call(
        pack_grads_kernel,
        out_shape=jax.ShapeDtypeStruct((EXPERTS, GROUP, CAP, gpiece), jnp.bfloat16),
        in_specs=[VMEM] * 5,
        out_specs=VMEM,
        compiler_params=params(),
        name="pack_grads",
    )(mod, idx, grad_hidden, pre_gate, pre_up)
    g_send, activations, shard = lax.optimization_barrier((g_send, activations, master))
    g_recv = lax.all_to_all(
        g_send.reshape(members, CAP, gpiece), EXP, split_axis=0, concat_axis=0, tiled=True
    )
    own_bf = shard.astype(jnp.bfloat16)
    came_bf = lax.ppermute(own_bf, "xh", swap_pairs(2))
    pair_bf = jnp.where(
        half == 0,
        jnp.concatenate([own_bf, came_bf], axis=0),
        jnp.concatenate([came_bf, own_bf], axis=0),
    )
    x_send, routing = pl.pallas_call(
        pack_rows_kernel,
        out_shape=(
            jax.ShapeDtypeStruct((EXPERTS, GROUP, CAP, piece), jnp.bfloat16),
            jax.ShapeDtypeStruct((EXPERTS * CAP, tok_count), jnp.bfloat16),
        ),
        in_specs=[VMEM] * 3,
        out_specs=(VMEM, VMEM),
        compiler_params=params(FULL),
        name="pack_rows",
    )(mod, idx, activations)
    g_recv, x_send, pair_late = lax.optimization_barrier((g_recv, x_send, pair_bf))
    g_mine = g_recv.reshape(rows_total, gpiece)
    g_all = lax.all_gather(
        g_mine,
        EXP,
        axis=0,
        tiled=False,
        axis_index_groups=[list(range(GROUP * e, GROUP * (e + 1))) for e in range(EXPERTS)],
    )
    x_recv = lax.all_to_all(
        x_send.reshape(members, CAP, piece), EXP, split_axis=0, concat_axis=0, tiled=True
    )
    x_rows = x_recv.reshape(rows_total, piece)
    shards = [pair_bf]
    for k in range(1, RING):
        moved = pair_bf if k in EARLY else pair_late
        shards.append(lax.ppermute(moved, "z", [(i, (i + k) % RING) for i in range(RING)]))
    x_turned = pl.pallas_call(
        turn_kernel,
        out_shape=pltpu.VMEM((piece, rows_total), jnp.bfloat16),
        in_specs=[VMEM],
        out_specs=VMEM,
        compiler_params=params(),
        name="turn",
    )(pltpu.with_memory_space_constraint(x_rows, pltpu.VMEM))
    g_all, *shards = lax.optimization_barrier((g_all, *shards))

    grad_part = pl.pallas_call(
        weight_grad_kernel,
        out_shape=jax.ShapeDtypeStruct((piece, 2 * hidden), jnp.bfloat16),
        in_specs=[VMEM, anywhere],
        out_specs=anywhere,
        scratch_shapes=[
            pltpu.VMEM((GROUP, rows_total, gpiece), jnp.bfloat16),
            pltpu.VMEM((piece, 2 * hidden), jnp.bfloat16),
            pltpu.SemaphoreType.DMA((GROUP // 2,)),
            pltpu.SemaphoreType.DMA((GROUP // 2,)),
        ],
        compiler_params=params(),
        name="weight_grad",
    )(pltpu.with_memory_space_constraint(x_turned, pltpu.VMEM), g_all)
    grad_z = lax.psum_scatter(grad_part, "z", scatter_dimension=0, tiled=True)

    grad_part, g_all, *shards = lax.optimization_barrier((grad_part, g_all, *shards))
    dx_rows = pl.pallas_call(
        input_grad_kernel,
        out_shape=jax.ShapeDtypeStruct((rows_total, piece), jnp.bfloat16),
        in_specs=[pl.BlockSpec(memory_space=pltpu.SMEM)] + [anywhere] * (RING + 1),
        out_specs=anywhere,
        scratch_shapes=[
            pltpu.VMEM((GROUP, rows_total, gpiece), jnp.bfloat16),
            pltpu.VMEM((piece, 2 * hidden), jnp.bfloat16),
            pltpu.VMEM((rows_total, piece), jnp.bfloat16),
            pltpu.SemaphoreType.DMA((DX_BLOCKS,)),
            pltpu.SemaphoreType.DMA((RING,)),
            pltpu.SemaphoreType.DMA((DX_BLOCKS,)),
        ],
        compiler_params=params(),
        name="input_grad",
    )(place, g_all, *shards)
    back = lax.all_to_all(
        dx_rows.reshape(members, CAP, piece), EXP, split_axis=0, concat_axis=0, tiled=True
    )
    input_grad = pl.pallas_call(
        combine_kernel,
        out_shape=jax.ShapeDtypeStruct((tok_count, width), jnp.bfloat16),
        in_specs=[VMEM] * 2,
        out_specs=anywhere,
        scratch_shapes=[
            pltpu.VMEM((tok_count, width), jnp.bfloat16),
            pltpu.SemaphoreType.DMA((GROUP,)),
        ],
        compiler_params=params(),
        name="combine",
    )(
        routing,
        pltpu.with_memory_space_constraint(
            back.reshape(EXPERTS, GROUP, CAP, piece), pltpu.VMEM
        ),
    )

    keep_rows = master.shape[0]
    halves = grad_z.reshape(2, keep_rows, 2 * hidden)
    own = lax.dynamic_index_in_dim(halves, half, 0, keepdims=False)
    other = lax.dynamic_index_in_dim(halves, 1 - half, 0, keepdims=False)
    came = lax.ppermute(other, "xh", swap_pairs(2))
    weight_grad = own.astype(jnp.float32) + came.astype(jnp.float32)
    new_first = beta_one * first_moment + (1.0 - beta_one) * weight_grad
    new_second = beta_two * second_moment + (1.0 - beta_two) * weight_grad * weight_grad
    corr_one = 1.0 - beta_one**adam_count
    corr_two = 1.0 - beta_two**adam_count
    update = new_first / corr_one / (jnp.sqrt(new_second / corr_two) + adam_eps)
    new_master = master - learn_rate * update
    return (input_grad, new_master, new_first, new_second)


def solution(mesh):
    fine = Mesh(mesh.devices.reshape(8, 2, 8, 2, 2), ALL)
    tok = P(ALL, None)
    par = P(EXP + REP, None)
    in_specs = (tok, tok, tok, tok, P(ALL), P(ALL), par, par, par)
    out_specs = (tok, par, par, par)
    return jax.shard_map(body, mesh=fine, in_specs=in_specs, out_specs=out_specs, check_vma=False)
```

```python
import jax
import jax.numpy as jnp
from jax import lax
from jax.experimental import pallas as pl
from jax.experimental.pallas import tpu as pltpu
from jax.sharding import Mesh, PartitionSpec as P

EXPERTS = 4
CAP = 48
GROUP = 8
RING = 8
DX_BLOCKS = 3
EARLY = (3, 4)

beta_one = 0.9
beta_two = 0.999
learn_rate = 0.02
adam_eps = 1e-08
adam_count = 1000

REP = ("z", "xh")
EXP = ("y", "xl", "core")
ALL = REP + EXP
VMEM = pl.BlockSpec(memory_space=pltpu.VMEM)
BIG = 56 * 1024 * 1024
FULL = 63 * 1024 * 1024 + 512 * 1024


def params(limit=BIG):
    return pltpu.CompilerParams(vmem_limit_bytes=limit)


def routing_rows(mod_ref, idx_ref):
    expert = 2 * mod_ref[...] + idx_ref[...]
    count = expert.shape[1]
    onehot = (
        lax.broadcasted_iota(jnp.int32, (8, count), 0) == jnp.broadcast_to(expert, (8, count))
    ).astype(jnp.bfloat16)
    earlier = (
        lax.broadcasted_iota(jnp.int32, (count, count), 0)
        < lax.broadcasted_iota(jnp.int32, (count, count), 1)
    ).astype(jnp.bfloat16)
    before = jnp.dot(onehot, earlier, preferred_element_type=jnp.float32)
    pos = jnp.sum(before * onehot.astype(jnp.float32), axis=0, keepdims=True).astype(jnp.int32)
    slot = lax.broadcasted_iota(jnp.int32, (CAP, count), 0)
    rows = [
        jnp.where((slot == pos) & (expert == e), 1.0, 0.0).astype(jnp.bfloat16)
        for e in range(EXPERTS)
    ]
    return rows


def pack_grads_kernel(mod_ref, idx_ref, grad_ref, gate_ref, up_ref, out_ref):
    rows = routing_rows(mod_ref, idx_ref)
    routing = jnp.concatenate(rows, axis=0)
    hidden = grad_ref.shape[1]
    piece = out_ref.shape[3]
    for start in range(0, hidden, piece):
        cols = pl.ds(start, piece)
        grad_val = grad_ref[:, cols].astype(jnp.float32)
        gate_val = gate_ref[:, cols].astype(jnp.float32)
        up_val = up_ref[:, cols].astype(jnp.float32)
        sig = 1.0 / (1.0 + jnp.exp(-gate_val))
        grad_gate = (grad_val * up_val * sig * (1.0 + gate_val * (1.0 - sig))).astype(jnp.bfloat16)
        grad_up = (grad_val * gate_val * sig).astype(jnp.bfloat16)
        g = start // piece
        for at, block in ((g, grad_gate), (g + GROUP // 2, grad_up)):
            packed = jnp.dot(routing, block, preferred_element_type=jnp.float32)
            packed = packed.astype(jnp.bfloat16)
            for e in range(EXPERTS):
                out_ref[e, at] = packed[e * CAP : (e + 1) * CAP]


def pack_rows_kernel(mod_ref, idx_ref, x_ref, out_ref, routing_ref):
    routing = jnp.concatenate(routing_rows(mod_ref, idx_ref), axis=0)
    routing_ref[...] = routing
    piece = out_ref.shape[3]
    for g in range(GROUP):
        block = x_ref[:, g * piece : (g + 1) * piece]
        packed = jnp.dot(routing, block, preferred_element_type=jnp.float32).astype(jnp.bfloat16)
        for e in range(EXPERTS):
            out_ref[e, g] = packed[e * CAP : (e + 1) * CAP]


def combine_kernel(routing_ref, back_ref, out_ref, out_buf, sems):
    routing = routing_ref[...]
    piece = back_ref.shape[3]
    stores = []
    for g in range(GROUP):
        block = jnp.concatenate([back_ref[e, g] for e in range(EXPERTS)], axis=0)
        total = lax.dot_general(
            routing, block, (((0,), (0,)), ((), ())), preferred_element_type=jnp.float32
        )
        cols = pl.ds(g * piece, piece)
        out_buf[:, cols] = total.astype(jnp.bfloat16)
        stores.append(
            pltpu.make_async_copy(out_buf.at[:, cols], out_ref.at[:, cols], sems.at[g])
        )
        stores[-1].start()
    for store in stores:
        store.wait()


def turn_kernel(x_ref, xt_ref):
    xt_ref[...] = x_ref[...].T


def weight_grad_kernel(xt_ref, g_ref, dw_ref, g_buf, dw_buf, g_sems, out_sems):
    pairs = GROUP // 2
    loads = [
        pltpu.make_async_copy(g_ref.at[pl.ds(2 * j, 2)], g_buf.at[pl.ds(2 * j, 2)], g_sems.at[j])
        for j in range(pairs)
    ]
    for load in loads[:-1]:
        load.start()
    stores = []
    piece = g_buf.shape[2]
    for j in range(pairs):
        loads[j].wait()
        if j == 0:
            loads[-1].start()
        pair = jnp.concatenate([g_buf[2 * j], g_buf[2 * j + 1]], axis=1)
        cols = slice(2 * j * piece, (2 * j + 2) * piece)
        dw_buf[:, cols] = jnp.dot(
            xt_ref[...], pair, preferred_element_type=jnp.float32
        ).astype(jnp.bfloat16)
        stores.append(
            pltpu.make_async_copy(dw_buf.at[:, cols], dw_ref.at[:, cols], out_sems.at[j])
        )
        stores[-1].start()
    for store in stores:
        store.wait()


def input_grad_kernel(z_ref, g_ref, *rest):
    shards, rest = rest[:RING], rest[RING:]
    dx_ref, g_buf, w_buf, dx_buf, g_sems, w_sems, out_sems = rest
    rows = shards[0].shape[0]
    w_loads = []
    for k in range(RING):
        at = pl.multiple_of(lax.rem(z_ref[0] + RING - k, RING) * rows, rows)
        w_loads.append(
            pltpu.make_async_copy(shards[k], w_buf.at[pl.ds(at, rows)], w_sems.at[k])
        )
    total = dx_buf.shape[0]
    edges = [0, total // 6, total * 7 // 12, total]
    parts = [slice(edges[j], edges[j + 1]) for j in range(DX_BLOCKS)]
    loads = [
        pltpu.make_async_copy(g_ref.at[:, part], g_buf.at[:, part], g_sems.at[j])
        for j, part in enumerate(parts)
    ]
    for load in w_loads + loads[:-1]:
        load.start()
    for load in w_loads:
        load.wait()
    stores = []
    for j, part in enumerate(parts):
        loads[j].wait()
        if j == 0:
            loads[-1].start()
        grads = jnp.concatenate([g_buf[g, part] for g in range(GROUP)], axis=1)
        dx_buf[part] = lax.dot_general(
            grads, w_buf[...], (((1,), (1,)), ((), ())), preferred_element_type=jnp.float32
        ).astype(jnp.bfloat16)
        stores.append(pltpu.make_async_copy(dx_buf.at[part], dx_ref.at[part], out_sems.at[j]))
        stores[-1].start()
    for store in stores:
        store.wait()


def swap_pairs(count):
    return [(i, i ^ 1) for i in range(count)]


def body(
    activations,
    grad_hidden,
    pre_gate,
    pre_up,
    modality,
    expert_index,
    master,
    first_moment,
    second_moment,
):
    tok_count, width = activations.shape
    hidden = grad_hidden.shape[1]
    piece = width // GROUP
    gpiece = 2 * hidden // GROUP
    members = EXPERTS * GROUP
    rows_total = members * CAP
    mod = modality.reshape(1, tok_count)
    idx = expert_index.reshape(1, tok_count)
    half = lax.axis_index("xh")
    place = lax.axis_index("z").astype(jnp.int32).reshape(1)

    anywhere = pl.BlockSpec(memory_space=pl.ANY)
    anywhere = pl.BlockSpec(memory_space=pl.ANY)
    g_send = pl.pallas_call(
        pack_grads_kernel,
        out_shape=jax.ShapeDtypeStruct((EXPERTS, GROUP, CAP, gpiece), jnp.bfloat16),
        in_specs=[VMEM] * 5,
        out_specs=VMEM,
        compiler_params=params(),
        name="pack_grads",
    )(mod, idx, grad_hidden, pre_gate, pre_up)
    g_send, activations, shard = lax.optimization_barrier((g_send, activations, master))
    g_recv = lax.all_to_all(
        g_send.reshape(members, CAP, gpiece), EXP, split_axis=0, concat_axis=0, tiled=True
    )
    own_bf = shard.astype(jnp.bfloat16)
    came_bf = lax.ppermute(own_bf, "xh", swap_pairs(2))
    pair_bf = jnp.where(
        half == 0,
        jnp.concatenate([own_bf, came_bf], axis=0),
        jnp.concatenate([came_bf, own_bf], axis=0),
    )
    x_send, routing = pl.pallas_call(
        pack_rows_kernel,
        out_shape=(
            jax.ShapeDtypeStruct((EXPERTS, GROUP, CAP, piece), jnp.bfloat16),
            jax.ShapeDtypeStruct((EXPERTS * CAP, tok_count), jnp.bfloat16),
        ),
        in_specs=[VMEM] * 3,
        out_specs=(VMEM, VMEM),
        compiler_params=params(FULL),
        name="pack_rows",
    )(mod, idx, activations)
    g_recv, x_send, pair_late = lax.optimization_barrier((g_recv, x_send, pair_bf))
    g_mine = g_recv.reshape(rows_total, gpiece)
    g_all = lax.all_gather(
        g_mine,
        EXP,
        axis=0,
        tiled=False,
        axis_index_groups=[list(range(GROUP * e, GROUP * (e + 1))) for e in range(EXPERTS)],
    )
    x_recv = lax.all_to_all(
        x_send.reshape(members, CAP, piece), EXP, split_axis=0, concat_axis=0, tiled=True
    )
    x_rows = x_recv.reshape(rows_total, piece)
    shards = [pair_bf]
    for k in range(1, RING):
        moved = pair_bf if k in EARLY else pair_late
        shards.append(lax.ppermute(moved, "z", [(i, (i + k) % RING) for i in range(RING)]))
    x_turned = pl.pallas_call(
        turn_kernel,
        out_shape=pltpu.VMEM((piece, rows_total), jnp.bfloat16),
        in_specs=[VMEM],
        out_specs=VMEM,
        compiler_params=params(),
        name="turn",
    )(pltpu.with_memory_space_constraint(x_rows, pltpu.VMEM))
    g_all, *shards = lax.optimization_barrier((g_all, *shards))

    grad_part = pl.pallas_call(
        weight_grad_kernel,
        out_shape=jax.ShapeDtypeStruct((piece, 2 * hidden), jnp.bfloat16),
        in_specs=[VMEM, anywhere],
        out_specs=anywhere,
        scratch_shapes=[
            pltpu.VMEM((GROUP, rows_total, gpiece), jnp.bfloat16),
            pltpu.VMEM((piece, 2 * hidden), jnp.bfloat16),
            pltpu.SemaphoreType.DMA((GROUP // 2,)),
            pltpu.SemaphoreType.DMA((GROUP // 2,)),
        ],
        compiler_params=params(),
        name="weight_grad",
    )(pltpu.with_memory_space_constraint(x_turned, pltpu.VMEM), g_all)
    grad_z = lax.psum_scatter(grad_part, "z", scatter_dimension=0, tiled=True)

    grad_part, g_all, *shards = lax.optimization_barrier((grad_part, g_all, *shards))
    near = [
        shard if k in EARLY else pltpu.with_memory_space_constraint(shard, pltpu.VMEM)
        for k, shard in enumerate(shards)
    ]
    dx_rows = pl.pallas_call(
        input_grad_kernel,
        out_shape=jax.ShapeDtypeStruct((rows_total, piece), jnp.bfloat16),
        in_specs=[pl.BlockSpec(memory_space=pltpu.SMEM), anywhere]
        + [anywhere if k in EARLY else VMEM for k in range(RING)],
        out_specs=anywhere,
        scratch_shapes=[
            pltpu.VMEM((GROUP, rows_total, gpiece), jnp.bfloat16),
            pltpu.VMEM((piece, 2 * hidden), jnp.bfloat16),
            pltpu.VMEM((rows_total, piece), jnp.bfloat16),
            pltpu.SemaphoreType.DMA((DX_BLOCKS,)),
            pltpu.SemaphoreType.DMA((RING,)),
            pltpu.SemaphoreType.DMA((DX_BLOCKS,)),
        ],
        compiler_params=params(),
        name="input_grad",
    )(place, g_all, *near)
    back = lax.all_to_all(
        dx_rows.reshape(members, CAP, piece), EXP, split_axis=0, concat_axis=0, tiled=True
    )
    input_grad = pl.pallas_call(
        combine_kernel,
        out_shape=jax.ShapeDtypeStruct((tok_count, width), jnp.bfloat16),
        in_specs=[VMEM] * 2,
        out_specs=anywhere,
        scratch_shapes=[
            pltpu.VMEM((tok_count, width), jnp.bfloat16),
            pltpu.SemaphoreType.DMA((GROUP,)),
        ],
        compiler_params=params(),
        name="combine",
    )(
        routing,
        pltpu.with_memory_space_constraint(
            back.reshape(EXPERTS, GROUP, CAP, piece), pltpu.VMEM
        ),
    )

    keep_rows = master.shape[0]
    halves = grad_z.reshape(2, keep_rows, 2 * hidden)
    own = lax.dynamic_index_in_dim(halves, half, 0, keepdims=False)
    other = lax.dynamic_index_in_dim(halves, 1 - half, 0, keepdims=False)
    came = lax.ppermute(other, "xh", swap_pairs(2))
    weight_grad = own.astype(jnp.float32) + came.astype(jnp.float32)
    new_first = beta_one * first_moment + (1.0 - beta_one) * weight_grad
    new_second = beta_two * second_moment + (1.0 - beta_two) * weight_grad * weight_grad
    corr_one = 1.0 - beta_one**adam_count
    corr_two = 1.0 - beta_two**adam_count
    update = new_first / corr_one / (jnp.sqrt(new_second / corr_two) + adam_eps)
    new_master = master - learn_rate * update
    return (input_grad, new_master, new_first, new_second)


def solution(mesh):
    fine = Mesh(mesh.devices.reshape(8, 2, 8, 2, 2), ALL)
    tok = P(ALL, None)
    par = P(EXP + REP, None)
    in_specs = (tok, tok, tok, tok, P(ALL), P(ALL), par, par, par)
    out_specs = (tok, par, par, par)
    return jax.shard_map(body, mesh=fine, in_specs=in_specs, out_specs=out_specs, check_vma=False)
```

```python
import jax
import jax.numpy as jnp
from jax import lax
from jax.experimental import pallas as pl
from jax.experimental.pallas import tpu as pltpu
from jax.sharding import Mesh, PartitionSpec as P

EXPERTS = 4
CAP = 48
GROUP = 8
RING = 8
DX_BLOCKS = 3
EARLY = (3, 4)

beta_one = 0.9
beta_two = 0.999
learn_rate = 0.02
adam_eps = 1e-08
adam_count = 1000

REP = ("z", "xh")
EXP = ("y", "xl", "core")
ALL = REP + EXP
VMEM = pl.BlockSpec(memory_space=pltpu.VMEM)
BIG = 56 * 1024 * 1024
FULL = 63 * 1024 * 1024 + 512 * 1024


def params(limit=BIG):
    return pltpu.CompilerParams(vmem_limit_bytes=limit)


def routing_rows(mod_ref, idx_ref):
    expert = 2 * mod_ref[...] + idx_ref[...]
    count = expert.shape[1]
    onehot = (
        lax.broadcasted_iota(jnp.int32, (8, count), 0) == jnp.broadcast_to(expert, (8, count))
    ).astype(jnp.bfloat16)
    earlier = (
        lax.broadcasted_iota(jnp.int32, (count, count), 0)
        < lax.broadcasted_iota(jnp.int32, (count, count), 1)
    ).astype(jnp.bfloat16)
    before = jnp.dot(onehot, earlier, preferred_element_type=jnp.float32)
    pos = jnp.sum(before * onehot.astype(jnp.float32), axis=0, keepdims=True).astype(jnp.int32)
    slot = lax.broadcasted_iota(jnp.int32, (CAP, count), 0)
    rows = [
        jnp.where((slot == pos) & (expert == e), 1.0, 0.0).astype(jnp.bfloat16)
        for e in range(EXPERTS)
    ]
    return rows


def pack_grads_kernel(mod_ref, idx_ref, grad_ref, gate_ref, up_ref, out_ref):
    rows = routing_rows(mod_ref, idx_ref)
    routing = jnp.concatenate(rows, axis=0)
    hidden = grad_ref.shape[1]
    piece = out_ref.shape[3]
    for start in range(0, hidden, piece):
        cols = pl.ds(start, piece)
        grad_val = grad_ref[:, cols].astype(jnp.float32)
        gate_val = gate_ref[:, cols].astype(jnp.float32)
        up_val = up_ref[:, cols].astype(jnp.float32)
        sig = 1.0 / (1.0 + jnp.exp(-gate_val))
        grad_gate = (grad_val * up_val * sig * (1.0 + gate_val * (1.0 - sig))).astype(jnp.bfloat16)
        grad_up = (grad_val * gate_val * sig).astype(jnp.bfloat16)
        g = start // piece
        for at, block in ((g, grad_gate), (g + GROUP // 2, grad_up)):
            packed = jnp.dot(routing, block, preferred_element_type=jnp.float32)
            packed = packed.astype(jnp.bfloat16)
            for e in range(EXPERTS):
                out_ref[e, at] = packed[e * CAP : (e + 1) * CAP]


def pack_rows_kernel(mod_ref, idx_ref, x_ref, out_ref, routing_ref):
    routing = jnp.concatenate(routing_rows(mod_ref, idx_ref), axis=0)
    routing_ref[...] = routing
    piece = out_ref.shape[3]
    for g in range(GROUP):
        block = x_ref[:, g * piece : (g + 1) * piece]
        packed = jnp.dot(routing, block, preferred_element_type=jnp.float32).astype(jnp.bfloat16)
        for e in range(EXPERTS):
            out_ref[e, g] = packed[e * CAP : (e + 1) * CAP]


def combine_kernel(routing_ref, back_ref, out_ref, out_buf, sems):
    routing = routing_ref[...]
    piece = back_ref.shape[3]
    stores = []
    for g in range(GROUP):
        block = jnp.concatenate([back_ref[e, g] for e in range(EXPERTS)], axis=0)
        total = lax.dot_general(
            routing, block, (((0,), (0,)), ((), ())), preferred_element_type=jnp.float32
        )
        cols = pl.ds(g * piece, piece)
        out_buf[:, cols] = total.astype(jnp.bfloat16)
        stores.append(
            pltpu.make_async_copy(out_buf.at[:, cols], out_ref.at[:, cols], sems.at[g])
        )
        stores[-1].start()
    for store in stores:
        store.wait()


def turn_kernel(x_ref, xt_ref):
    xt_ref[...] = x_ref[...].T


def weight_grad_kernel(xt_ref, g_ref, dw_ref, g_buf, dw_buf, g_sems, out_sems):
    pairs = GROUP // 2
    loads = [
        pltpu.make_async_copy(g_ref.at[pl.ds(2 * j, 2)], g_buf.at[pl.ds(2 * j, 2)], g_sems.at[j])
        for j in range(pairs)
    ]
    for load in loads[:-1]:
        load.start()
    stores = []
    piece = g_buf.shape[2]
    for j, (first, last) in enumerate(((0, 1), (1, 2), (2, pairs))):
        for load in loads[first:last]:
            load.wait()
        if j == 0:
            loads[-1].start()
        wide = jnp.concatenate([g_buf[i] for i in range(2 * first, 2 * last)], axis=1)
        cols = slice(2 * first * piece, 2 * last * piece)
        dw_buf[:, cols] = jnp.dot(
            xt_ref[...], wide, preferred_element_type=jnp.float32
        ).astype(jnp.bfloat16)
        stores.append(
            pltpu.make_async_copy(dw_buf.at[:, cols], dw_ref.at[:, cols], out_sems.at[j])
        )
        stores[-1].start()
    for store in stores:
        store.wait()


def input_grad_kernel(z_ref, g_ref, *rest):
    shards, rest = rest[:RING], rest[RING:]
    dx_ref, g_buf, w_buf, dx_buf, g_sems, w_sems, out_sems = rest
    rows = shards[0].shape[0]
    w_loads = []
    for k in range(RING):
        at = pl.multiple_of(lax.rem(z_ref[0] + RING - k, RING) * rows, rows)
        w_loads.append(
            pltpu.make_async_copy(shards[k], w_buf.at[pl.ds(at, rows)], w_sems.at[k])
        )
    total = dx_buf.shape[0]
    edges = [0, total // 6, total * 7 // 12, total]
    parts = [slice(edges[j], edges[j + 1]) for j in range(DX_BLOCKS)]
    loads = [
        pltpu.make_async_copy(g_ref.at[:, part], g_buf.at[:, part], g_sems.at[j])
        for j, part in enumerate(parts)
    ]
    for load in w_loads + loads[:-1]:
        load.start()
    for load in w_loads:
        load.wait()
    stores = []
    for j, part in enumerate(parts):
        loads[j].wait()
        if j == 0:
            loads[-1].start()
        grads = jnp.concatenate([g_buf[g, part] for g in range(GROUP)], axis=1)
        dx_buf[part] = lax.dot_general(
            grads, w_buf[...], (((1,), (1,)), ((), ())), preferred_element_type=jnp.float32
        ).astype(jnp.bfloat16)
        stores.append(pltpu.make_async_copy(dx_buf.at[part], dx_ref.at[part], out_sems.at[j]))
        stores[-1].start()
    for store in stores:
        store.wait()


def swap_pairs(count):
    return [(i, i ^ 1) for i in range(count)]


def body(
    activations,
    grad_hidden,
    pre_gate,
    pre_up,
    modality,
    expert_index,
    master,
    first_moment,
    second_moment,
):
    tok_count, width = activations.shape
    hidden = grad_hidden.shape[1]
    piece = width // GROUP
    gpiece = 2 * hidden // GROUP
    members = EXPERTS * GROUP
    rows_total = members * CAP
    mod = modality.reshape(1, tok_count)
    idx = expert_index.reshape(1, tok_count)
    half = lax.axis_index("xh")
    place = lax.axis_index("z").astype(jnp.int32).reshape(1)

    anywhere = pl.BlockSpec(memory_space=pl.ANY)
    anywhere = pl.BlockSpec(memory_space=pl.ANY)
    g_send = pl.pallas_call(
        pack_grads_kernel,
        out_shape=jax.ShapeDtypeStruct((EXPERTS, GROUP, CAP, gpiece), jnp.bfloat16),
        in_specs=[VMEM] * 5,
        out_specs=VMEM,
        compiler_params=params(),
        name="pack_grads",
    )(mod, idx, grad_hidden, pre_gate, pre_up)
    g_send, activations, shard = lax.optimization_barrier((g_send, activations, master))
    g_recv = lax.all_to_all(
        g_send.reshape(members, CAP, gpiece), EXP, split_axis=0, concat_axis=0, tiled=True
    )
    own_bf = shard.astype(jnp.bfloat16)
    came_bf = lax.ppermute(own_bf, "xh", swap_pairs(2))
    pair_bf = jnp.where(
        half == 0,
        jnp.concatenate([own_bf, came_bf], axis=0),
        jnp.concatenate([came_bf, own_bf], axis=0),
    )
    x_send, routing = pl.pallas_call(
        pack_rows_kernel,
        out_shape=(
            jax.ShapeDtypeStruct((EXPERTS, GROUP, CAP, piece), jnp.bfloat16),
            jax.ShapeDtypeStruct((EXPERTS * CAP, tok_count), jnp.bfloat16),
        ),
        in_specs=[VMEM] * 3,
        out_specs=(VMEM, VMEM),
        compiler_params=params(FULL),
        name="pack_rows",
    )(mod, idx, activations)
    g_recv, x_send, pair_late = lax.optimization_barrier((g_recv, x_send, pair_bf))
    g_mine = g_recv.reshape(rows_total, gpiece)
    g_all = lax.all_gather(
        g_mine,
        EXP,
        axis=0,
        tiled=False,
        axis_index_groups=[list(range(GROUP * e, GROUP * (e + 1))) for e in range(EXPERTS)],
    )
    x_recv = lax.all_to_all(
        x_send.reshape(members, CAP, piece), EXP, split_axis=0, concat_axis=0, tiled=True
    )
    x_rows = x_recv.reshape(rows_total, piece)
    shards = [pair_bf]
    for k in range(1, RING):
        moved = pair_bf if k in EARLY else pair_late
        shards.append(lax.ppermute(moved, "z", [(i, (i + k) % RING) for i in range(RING)]))
    x_turned = pl.pallas_call(
        turn_kernel,
        out_shape=pltpu.VMEM((piece, rows_total), jnp.bfloat16),
        in_specs=[VMEM],
        out_specs=VMEM,
        compiler_params=params(),
        name="turn",
    )(pltpu.with_memory_space_constraint(x_rows, pltpu.VMEM))
    g_all, *shards = lax.optimization_barrier((g_all, *shards))

    grad_part = pl.pallas_call(
        weight_grad_kernel,
        out_shape=jax.ShapeDtypeStruct((piece, 2 * hidden), jnp.bfloat16),
        in_specs=[VMEM, anywhere],
        out_specs=anywhere,
        scratch_shapes=[
            pltpu.VMEM((GROUP, rows_total, gpiece), jnp.bfloat16),
            pltpu.VMEM((piece, 2 * hidden), jnp.bfloat16),
            pltpu.SemaphoreType.DMA((GROUP // 2,)),
            pltpu.SemaphoreType.DMA((GROUP // 2,)),
        ],
        compiler_params=params(),
        name="weight_grad",
    )(pltpu.with_memory_space_constraint(x_turned, pltpu.VMEM), g_all)
    grad_z = lax.psum_scatter(grad_part, "z", scatter_dimension=0, tiled=True)

    grad_part, g_all, *shards = lax.optimization_barrier((grad_part, g_all, *shards))
    dx_rows = pl.pallas_call(
        input_grad_kernel,
        out_shape=jax.ShapeDtypeStruct((rows_total, piece), jnp.bfloat16),
        in_specs=[pl.BlockSpec(memory_space=pltpu.SMEM)] + [anywhere] * (RING + 1),
        out_specs=anywhere,
        scratch_shapes=[
            pltpu.VMEM((GROUP, rows_total, gpiece), jnp.bfloat16),
            pltpu.VMEM((piece, 2 * hidden), jnp.bfloat16),
            pltpu.VMEM((rows_total, piece), jnp.bfloat16),
            pltpu.SemaphoreType.DMA((DX_BLOCKS,)),
            pltpu.SemaphoreType.DMA((RING,)),
            pltpu.SemaphoreType.DMA((DX_BLOCKS,)),
        ],
        compiler_params=params(),
        name="input_grad",
    )(place, g_all, *shards)
    back = lax.all_to_all(
        dx_rows.reshape(members, CAP, piece), EXP, split_axis=0, concat_axis=0, tiled=True
    )
    input_grad = pl.pallas_call(
        combine_kernel,
        out_shape=jax.ShapeDtypeStruct((tok_count, width), jnp.bfloat16),
        in_specs=[VMEM] * 2,
        out_specs=anywhere,
        scratch_shapes=[
            pltpu.VMEM((tok_count, width), jnp.bfloat16),
            pltpu.SemaphoreType.DMA((GROUP,)),
        ],
        compiler_params=params(),
        name="combine",
    )(
        routing,
        pltpu.with_memory_space_constraint(
            back.reshape(EXPERTS, GROUP, CAP, piece), pltpu.VMEM
        ),
    )

    keep_rows = master.shape[0]
    halves = grad_z.reshape(2, keep_rows, 2 * hidden)
    own = lax.dynamic_index_in_dim(halves, half, 0, keepdims=False)
    other = lax.dynamic_index_in_dim(halves, 1 - half, 0, keepdims=False)
    came = lax.ppermute(other, "xh", swap_pairs(2))
    weight_grad = own.astype(jnp.float32) + came.astype(jnp.float32)
    new_first = beta_one * first_moment + (1.0 - beta_one) * weight_grad
    new_second = beta_two * second_moment + (1.0 - beta_two) * weight_grad * weight_grad
    corr_one = 1.0 - beta_one**adam_count
    corr_two = 1.0 - beta_two**adam_count
    update = new_first / corr_one / (jnp.sqrt(new_second / corr_two) + adam_eps)
    new_master = master - learn_rate * update
    return (input_grad, new_master, new_first, new_second)


def solution(mesh):
    fine = Mesh(mesh.devices.reshape(8, 2, 8, 2, 2), ALL)
    tok = P(ALL, None)
    par = P(EXP + REP, None)
    in_specs = (tok, tok, tok, tok, P(ALL), P(ALL), par, par, par)
    out_specs = (tok, par, par, par)
    return jax.shard_map(body, mesh=fine, in_specs=in_specs, out_specs=out_specs, check_vma=False)
```
